128 devices in a mesh: lat: 8 (over x, core), lon: 16 (over z, y).
Axes of the slice: x: 4, y: 4, z: 4, core: 2. Of those that a mesh axis runs over, the one named last changes fastest.
Arguments:
- background: float32 [12, 256, 2048], P(None, 'lat', 'lon'), may hold values from -6 to 6
- wind_lon: float32 [12, 256, 2048], P(None, 'lat', 'lon'), may hold values from -0.4 to 0.4
- wind_lat: float32 [12, 256, 2048], P(None, 'lat', 'lon'), may hold values from -0.3 to 0.3
- obs_value: float32 [262144], P(('lat', 'lon')), may hold values from -6 to 6
- obs_weight: float32 [262144], P(('lat', 'lon')), may hold values from 0.25 to 4
- obs_tile: int32 [262144, 1], P(('lat', 'lon')), may hold values from 0 to 127; in each aligned block of 2048 rows (0 to 2047, 2048 to 4095, ...) at most 32 rows name the same one
- obs_cell: int32 [262144], P(('lat', 'lon')), may hold values from 0 to 49151
- obs_step: int32 [262144], P(('lat', 'lon')), may hold values from 1 to 4
- obs_count: int32 [128], P(('lat', 'lon')), may hold values from 512 to 2048, as said below
Outputs:
- increment: float32 [12, 256, 2048], P(None, 'lat', 'lon')
- residual: float32 [12, 256, 2048], P(None, 'lat', 'lon')
The draws below stay inside these ranges and needn't reach their ends.
Inputs may be any that keep to these rules, and one draw needn't show every extreme that they name: `obs_tile`: counted with lat slowest. Among the 2048 slots of one device at most 32 name the same tile, and in every draw some tile is named by exactly 32 slots of one device. `obs_cell`: level slowest, then latitude row, then longitude column within the tile. `obs_count`: slots of a device at or beyond its count are unused; in every draw some device has all 2048 slots live.
All inputs are finite; a program needn't handle non-finite values.
Results may differ from the reference program's by a relative error of at most 0.0012.
Values sent between devices are 32-bit elements; how exact they have to be, the bound alone decides.
No kernel may reach another device: no remote copies, remote signals or barrier semaphores. Data moves between devices by JAX's collectives and lax.ppermute only.
A program may use at most 64 MiB of HBM per device.

```python
import math
import jax
import jax.numpy as jnp
import numpy as np

CLAT = 32
CLON = 128
LEV = 12
STEPS = 4
ITERS = 2
OBS_DEV = 2048
CAP = 32
NLAT = 256
NLON = 2048
NOBS = 262144
N_LON = 16
DEVICES = 128


def draw_obs_count(key, part):
    counts = jax.random.randint(key, (DEVICES,), OBS_DEV // 4, OBS_DEV + 1)
    chosen = jax.random.randint(jax.random.fold_in(key, 7), (), 0, DEVICES)
    return jnp.where(jnp.arange(DEVICES) == chosen, OBS_DEV, counts).astype(jnp.int32)


def place_ends(array, stream_key, smallest, high):
    index_at = [jax.random.randint(jax.random.fold_in(stream_key, axis), (), 0, length) for axis, length in enumerate(array.shape)]
    main_axis = array.shape.index(max(array.shape))
    neighbour = index_at[:main_axis] + [(index_at[main_axis] + 1) % array.shape[main_axis]] + index_at[main_axis + 1:]
    return array.at[tuple(index_at)].set(smallest).at[tuple(neighbour)].set(high)


def shard_levels(own_key, extent, cuts, smallest, high):
    level, own = 1.0, jax.random.fold_in(own_key, 6)
    for dim, shards_of in cuts:
        draws = jnp.exp(jax.random.uniform(jax.random.fold_in(own, dim), (shards_of,), jnp.float32, smallest / len(cuts), high / len(cuts)))
        level = level * jnp.repeat(draws, extent[dim] // shards_of).reshape([-1 if axis == dim else 1 for axis in range(len(extent))])
    return level


def routed_block(key, own, number, rows, number_of, top, limit, lean):
    sequence = jax.random.permutation(key, number_of)
    packed, ordinary = shares(number_of, rows * top, limit, lean, True), shares(number_of, rows * top, limit, lean, False)
    places = jnp.arange(number_of)

    def named(sizes, rotation):
        used = int((sizes > 0).sum())
        fixed = max(1, used // 4)
        shifted = fixed + (places - fixed + rotation * (used - fixed)) % max(1, number_of - fixed)
        return jnp.zeros((number_of,), jnp.int32).at[sequence[jnp.where(places < fixed, places, shifted)]].set(jnp.asarray(sizes, jnp.int32))

    sizes = jnp.where(number % 4 == 0, named(packed, number // 4), named(ordinary, number - number // 4 - 1))
    mixed = jax.random.permutation(jax.random.fold_in(own, 3), number_of)
    donor, taker = mixed[0:number_of // 2 * 2:2], mixed[1:number_of // 2 * 2:2]
    margin = jnp.minimum(sizes[donor] - 1, limit - sizes[taker]) // 2
    margin = jnp.where((donor == sequence[0]) | (taker == sequence[0]) | (sizes[taker] == 0), 0, jnp.maximum(margin, 0))
    shifted = jax.random.randint(jax.random.fold_in(own, 4), (number_of // 2,), 0, 1 << 20) % (margin + 1)
    sizes = sizes.at[donor].add(-shifted).at[taker].add(shifted)
    items = jnp.searchsorted(jnp.cumsum(sizes), jnp.arange(rows * top), side="right").astype(jnp.int32)
    grid = items.reshape(top, rows).T
    grid = grid[jax.random.permutation(jax.random.fold_in(own, 1), rows)]
    rotation = jax.random.randint(jax.random.fold_in(own, 2), (rows, 1), 0, top)
    return jnp.take_along_axis(grid, (jnp.arange(top)[None, :] + rotation) % top, axis=1)


def shares(count, total, reach, slope, full):
    portions = [(1 << 20) // math.isqrt(grade ** slope) + 1 for grade in range(1, count + 1)]
    largest = reach if full else min(reach, max(-(-total // count), total * portions[0] // sum(portions)))
    least = 1 if total - largest >= count - 1 else 0
    holding, surplus = [largest] + [least] * (count - 1), total - largest - least * (count - 1)
    while surplus > 0:
        free = [i for i in range(1, count) if holding[i] < largest] or [i for i in range(1, count) if holding[i] < reach]
        mass, budget = sum([portions[i] for i in free]), surplus
        for i in free:
            extra = min(reach - holding[i], max(1, budget * portions[i] // mass), surplus)
            holding[i] = holding[i] + extra
            surplus = surplus - extra
    return np.array(holding)


def bell_draw(rng, shape, scale, bound, pieces=(), kind=jnp.bfloat16):
    entries = jax.random.normal(rng, shape, jnp.float32) * scale
    if len(pieces) > 0:
        entries = shard_levels(rng, shape, pieces, -0.22, 0.18) * entries
    return jnp.clip(entries, min=-bound, max=bound).astype(kind)


def setup_inputs(seed: int = 0) -> dict:
    streams_of = jax.random.split(jax.random.key(seed), 10)
    background = bell_draw(streams_of[0], (LEV, NLAT, NLON), 1.0, 6.0, ((1, 8), (2, 16)), jnp.float32)
    wind_lon = jnp.clip(jax.random.uniform(streams_of[1], (LEV, NLAT, NLON), jnp.float32, -0.4, 0.4) * shard_levels(streams_of[1], (LEV, NLAT, NLON), ((1, 8), (2, 16)), -0.4, 0.0), -0.4, 0.4)
    wind_lat = jnp.clip(jax.random.uniform(streams_of[2], (LEV, NLAT, NLON), jnp.float32, -0.3, 0.3) * shard_levels(streams_of[2], (LEV, NLAT, NLON), ((1, 8), (2, 16)), -0.4, 0.0), -0.3, 0.3)
    obs_value = bell_draw(streams_of[3], (NOBS,), 1.0, 6.0, ((0, 128),), jnp.float32)
    obs_weight = jnp.clip(jnp.exp(math.log(4.0) - 2.7725887 * jax.random.uniform(streams_of[4], (NOBS,), jnp.float32) ** shard_levels(streams_of[4], (NOBS,), ((0, 128),), -0.2, 0.2)), 0.25, 4.0)
    obs_tile_keys = jax.random.split(jax.random.fold_in(streams_of[5], 1), NOBS // OBS_DEV)
    obs_tile_turns = jax.random.permutation(jax.random.fold_in(streams_of[5], 3), NOBS // OBS_DEV)
    obs_tile = jax.vmap(lambda own, number: routed_block(jax.random.fold_in(streams_of[5], 2), own, number, OBS_DEV, DEVICES, 1, CAP, 2))(obs_tile_keys, obs_tile_turns).reshape((NOBS, 1))
    obs_cell = place_ends(jax.random.randint(streams_of[6], (NOBS,), 0, LEV * CLAT * CLON), jax.random.fold_in(streams_of[6], 1), 0, (LEV * CLAT * CLON) - 1).astype(jnp.int32)
    obs_step = place_ends(jax.random.randint(streams_of[7], (NOBS,), 1, STEPS + 1), jax.random.fold_in(streams_of[7], 1), 1, STEPS).astype(jnp.int32)
    obs_count = draw_obs_count(jax.random.fold_in(streams_of[9], 71), 0)
    return {"background": background, "wind_lon": wind_lon, "wind_lat": wind_lat, "obs_value": obs_value, "obs_weight": obs_weight, "obs_tile": obs_tile, "obs_cell": obs_cell, "obs_step": obs_step, "obs_count": obs_count}


shear_rate = 0.2
diffusion = 0.08


def pad_global(source):
    source = jnp.pad(source, ((0, 0), (1, 1), (0, 0)))
    return jnp.concatenate([source[:, :, -1:], source, source[:, :, :1]], axis=2)


def along_lon(padded):
    return 0.5 * (padded[:, 1:-1, 2:] - padded[:, 1:-1, :-2])


def along_lat(padded):
    return 0.5 * (padded[:, 2:, 1:-1] - padded[:, :-2, 1:-1])


def spread(padded):
    return (padded[:, 2:, 1:-1] + padded[:, :-2, 1:-1] + padded[:, 1:-1, 2:]
            + padded[:, 1:-1, :-2] - 4.0 * padded[:, 1:-1, 1:-1])


def reference(background, wind_lon, wind_lat, obs_value, obs_weight, obs_tile, obs_cell, obs_step, obs_count):
    plane = CLAT * CLON
    target = obs_tile[:, 0]
    within = obs_cell % plane
    lat_row = (target // N_LON) * CLAT + within // CLON
    lon_col = (target % N_LON) * CLON + within % CLON
    flat_cell = (((obs_cell // plane) * NLAT + lat_row) * NLON + lon_col).astype(jnp.int32)
    holder = jnp.arange(NOBS, dtype=jnp.int32) // OBS_DEV
    slot_no = jnp.arange(NOBS, dtype=jnp.int32) % OBS_DEV
    weights = jnp.where(slot_no < obs_count[holder], obs_weight, 0.0)

    states = [background]
    for moment in range(STEPS):
        current = states[-1]
        padded = pad_global(current)
        drift = wind_lon + shear_rate * current
        states.append(current - drift * along_lon(padded) - wind_lat * along_lat(padded)
                      + diffusion * spread(padded))

    observed = jnp.zeros((NOBS,), jnp.float32)
    for moment in range(STEPS):
        observed = observed + jnp.where(obs_step == moment + 1, states[moment + 1].reshape(-1)[flat_cell], 0.0)
    departures = obs_value - observed

    def forward_tangent(start):
        moving = start
        seen = jnp.zeros((NOBS,), jnp.float32)
        for moment in range(STEPS):
            current = states[moment]
            gain = 1.0 - shear_rate * along_lon(pad_global(current))
            drift = wind_lon + shear_rate * current
            padded = pad_global(moving)
            moving = (gain * moving - drift * along_lon(padded) - wind_lat * along_lat(padded)
                      + diffusion * spread(padded))
            seen = seen + jnp.where(obs_step == moment + 1, moving.reshape(-1)[flat_cell], 0.0)
        return seen

    def backward_adjoint(amounts):
        adjoint = jnp.zeros_like(background)
        for moment in reversed(range(STEPS)):
            adjoint = adjoint.reshape(-1).at[flat_cell].add(
                jnp.where(obs_step == moment + 1, amounts, 0.0)).reshape(background.shape)
            current = states[moment]
            gain = 1.0 - shear_rate * along_lon(pad_global(current))
            drift = wind_lon + shear_rate * current
            adjoint = (gain * adjoint + along_lon(pad_global(drift * adjoint))
                       + along_lat(pad_global(wind_lat * adjoint)) + diffusion * spread(pad_global(adjoint)))
        return adjoint

    def hessian(probe):
        return probe + backward_adjoint(weights * forward_tangent(probe))

    gradient = backward_adjoint(weights * departures)
    increment = jnp.zeros_like(background)
    residual = gradient
    direction = gradient
    norm_now = jnp.sum(residual * residual)
    for repeat in range(ITERS):
        image = hessian(direction)
        alpha = norm_now / jnp.sum(direction * image)
        increment = increment + alpha * direction
        residual = residual - alpha * image
        norm_next = jnp.sum(residual * residual)
        direction = residual + (norm_next / norm_now) * direction
        norm_now = norm_next
    return increment, residual
```

```python
import jax
import jax.numpy as jnp
from jax import lax
from jax.experimental import pallas as pl
from jax.experimental.pallas import tpu as pltpu
from jax.sharding import PartitionSpec as P

LAT = 8
LON = 16
ALL = 128
STEPS = 4
LV = 3
COL = 64
EDGE = 8
EXT = COL + 2 * EDGE
ROOM = 256
ROWS = STEPS * LV * COL
F32 = jnp.float32
BF16 = jnp.bfloat16
I32 = jnp.int32


def lanes(shape):
    return lax.broadcasted_iota(I32, shape, len(shape) - 1)


def sublanes(shape):
    return lax.broadcasted_iota(I32, shape, len(shape) - 2)


def half():
    return lax.rem(lax.axis_index("lat"), 2)


def prep_kernel(bg, wl, wt, out):
    low = lanes((16, 128)) < 64
    for f, ref in enumerate((bg, wl, wt)):
        for level in range(12):
            q, l = level // 3, level % 3
            even = ref[level, pl.ds(0, 16, stride=2), :]
            odd = ref[level, pl.ds(1, 16, stride=2), :]
            out[2 * q, f * 3 + l] = jnp.where(low, even, pltpu.roll(odd, 64, 1))
            out[2 * q + 1, f * 3 + l] = jnp.where(low, pltpu.roll(even, 64, 1), odd)


def put_edges(sa, sb, index, lo, hi, h):
    @pl.when(h == 0)
    def _():
        sa[index] = hi
        sb[index] = lo

    @pl.when(h != 0)
    def _():
        sa[index] = lo
        sb[index] = hi


def get_edges(ra, rb, index, h):
    a, b = ra[index], rb[index]
    first = jnp.full(a.shape, h, I32) == 0
    return jnp.where(first, b, a), jnp.where(first, a, b)


def recv_kernel(x, center, sa, sb):
    h = half()
    for f in range(9):
        t = x[:, f].reshape(128, 128).T
        for u in range(2):
            center[f, u] = t[u * 64 : u * 64 + 64]
            put_edges(sa, sb, (f, u), t[u * 64 : u * 64 + 8], t[u * 64 + 56 : u * 64 + 64], h)


def up(x):
    return pltpu.roll(x, EXT - 1, 0)


def down(x):
    return pltpu.roll(x, 1, 0)


def north(e, o):
    return pltpu.roll(o, 1, 1), e


def south(e, o):
    return o, pltpu.roll(e, 127, 1)


def forward_kernel(center, ra, rb, states, gains, drifts, cn, cs):
    h = half()
    lane = lanes((EXT, 128))

    def ext(f, u):
        left, right = get_edges(ra, rb, (f, u), h)
        return jnp.concatenate([left, center[f, u], right], axis=0)

    for l in range(LV):
        s = [ext(l, u) for u in range(2)]
        wl = [ext(3 + l, u) for u in range(2)]
        wt = [ext(6 + l, u) for u in range(2)]
        n = [0.08 + 0.5 * wt[u] for u in range(2)]
        d = [0.08 - 0.5 * wt[u] for u in range(2)]
        n[0] = jnp.where(lane == 0, 0.0, n[0])
        d[1] = jnp.where(lane == 127, 0.0, d[1])
        for u in range(2):
            cn[l, u] = n[u]
            cs[l, u] = d[u]
        for k in range(STEPS):
            no, so = north(*s), south(*s)
            new = []
            for u in range(2):
                hi, lo = up(s[u]), down(s[u])
                drift = 0.5 * wl[u] + 0.1 * s[u]
                gains[k, l, u] = 0.68 - 0.1 * (hi - lo)
                drifts[k, l, u] = drift
                new.append(
                    0.68 * s[u] + 0.08 * (hi + lo) - drift * (hi - lo) + n[u] * no[u] + d[u] * so[u]
                )
            s = new
            for u in range(2):
                states[k, l, u] = s[u]


def tangent(e, g, d, n, s):
    no, so = north(*e), south(*e)
    out = []
    for u in range(2):
        hi, lo = up(e[u]), down(e[u])
        out.append(g[u] * e[u] + 0.08 * (hi + lo) - d[u] * (hi - lo) + n[u] * no[u] + s[u] * so[u])
    return out


def adjoint(x, g, d, n, s):
    no = north(s[0] * x[0], s[1] * x[1])
    so = south(n[0] * x[0], n[1] * x[1])
    out = []
    for u in range(2):
        flow = d[u] * x[u]
        wide = 0.08 * x[u]
        out.append(g[u] * x[u] + up(wide + flow) + down(wide - flow) + no[u] + so[u])
    return out


def pack_kernel(count, tile, cell, step, value, weight, out, rows, base, acc, bt):
    shape = (16, 128)
    live = sublanes(shape) * 128 + lanes(shape) < count[0]
    c, t = cell[...], tile[...]
    level = c >> 12
    q = (level >= 3).astype(I32) + (level >= 6).astype(I32) + (level >= 9).astype(I32)
    row = (c & 4095) >> 7
    col = c & 127
    lat = (t >> 4) * 32 + row
    dest = (2 * q + (col >> 6)) * LON + (t & 15)
    w = jnp.where(live, weight[...], 0.0)
    w0 = w.astype(BF16).astype(F32)
    w1 = (w - w0).astype(BF16).astype(F32)
    wv = (w0 + w1) * value[...]
    v0 = wv.astype(BF16).astype(F32)
    v1 = (wv - v0).astype(BF16).astype(F32)
    v2 = wv - v0 - v1
    zero = jnp.zeros(shape, F32)
    rows[0] = jnp.where(live, dest, -1).astype(F32)
    rows[1] = (((level - 3 * q) * 64 + (col & 63)) * 256).astype(F32)
    rows[2] = step[...].astype(F32)
    rows[3] = w0
    rows[4] = v0
    rows[5] = ((lat & 1) * 128 + (lat >> 1)).astype(F32)
    rows[6] = zero
    rows[7] = w1
    rows[8] = v1
    rows[9] = zero
    rows[10] = zero
    rows[11] = zero
    rows[12] = v2
    base[...] = jnp.zeros_like(base)
    acc[...] = jnp.zeros_like(acc)
    square = (128, 256)
    before = ((sublanes(square) < lanes(square)) | (lanes(square) >= 128)).astype(F32).astype(BF16)
    ids = sublanes((128, 128)).astype(F32)
    places = sublanes((ROOM, 128)).astype(F32)

    def block(b, carry):
        def line(i):
            return rows[i, pl.ds(b, 1), :]

        member = jnp.where(ids == line(0), 1.0, 0.0)
        member16 = member.astype(BF16)
        counted = jnp.dot(member16, before, preferred_element_type=F32)
        rank = jnp.sum(member * (counted[:, :128] + base[...]), axis=0, keepdims=True)
        base[...] += counted[:, 128:]
        here = places == rank
        for p in range(3):
            for ch in range(4):
                piece = jnp.where(here, line(1 + 4 * p + ch), 0.0).astype(BF16)
                for m in range(8):
                    at = m * 128 + ch * 32
                    bt[at : at + 32, p * 128 : p * 128 + 128] = piece[m * 32 : m * 32 + 32]
        three = jnp.concatenate([member16, member16, member16], axis=1)
        acc[...] += lax.dot_general(
            three, bt[...], (((1,), (1,)), ((), ())), preferred_element_type=F32
        )
        return carry

    lax.fori_loop(0, 16, block, 0)
    for m in range(8):
        out[:, m, :] = acc[:, m * 128 : m * 128 + 128]


def scatter_kernel(x, wsum, vsum, sa, sb, xt, at, bt, acc):
    h = half()
    most = jnp.max(x[...], axis=0)
    lane = lanes((8, 128))
    used = jnp.where((lane >= 32) & (lane < 64) & (most > 0.5), 1.0, 0.0)
    total = jnp.sum(used).astype(I32)
    acc[...] = jnp.zeros_like(acc)
    for m in range(8):

        @pl.when(total > 32 * m)
        def _():
            xt[m * 128 : m * 128 + 128, :] = x[:, m, :].T

    row_ids = sublanes((ROWS, 128))
    lat_ids = sublanes((256, 128))

    def group(g, carry):
        start = (g // 4) * 128 + (g % 4) * 8

        def part(ch):
            return xt[pl.ds(pl.multiple_of(start + ch * 32, 8), 8), :]

        cell = part(0).astype(I32)
        row = (part(1).astype(I32) - 1) * (LV * COL) + (cell >> 8)
        lat = cell & 255
        w = part(2)
        v = part(3)
        w0 = w.astype(BF16).astype(F32)
        w1 = w - w0
        v0 = v.astype(BF16).astype(F32)
        v1 = (v - v0).astype(BF16).astype(F32)
        v2 = v - v0 - v1
        for r in range(8):
            cols = slice(r * 128, r * 128 + 128)
            at[:, cols] = jnp.where(row_ids == row[r : r + 1], 1.0, 0.0).astype(BF16)
            here = lat_ids == lat[r : r + 1]
            for p, piece in enumerate((w0, w1, v0, v1, v2)):
                bt[p * 256 : p * 256 + 256, cols] = jnp.where(here, piece[r : r + 1], 0.0).astype(BF16)
        acc[...] += lax.dot_general(
            at[...], bt[...], (((1,), (1,)), ((), ())), preferred_element_type=F32
        )
        return carry

    lax.fori_loop(0, (total + 7) // 8, group, 0)
    low = sublanes((8, 128)) < 4
    for k in range(STEPS):
        for l in range(LV):
            for u in range(2):
                rows = slice((k * LV + l) * COL, (k * LV + l + 1) * COL)
                take = lambda p: acc[rows, p * 256 + u * 128 : p * 256 + u * 128 + 128]
                w = take(0) + take(1)
                v = take(2) + take(3) + take(4)
                wsum[k, l, u] = w
                vsum[k, l, u] = v
                lo = jnp.where(low, w[:8], pltpu.roll(v[:8], 4, 0))
                hi = jnp.where(low, pltpu.roll(v[56:], 4, 0), w[56:])
                put_edges(sa, sb, (k, l, u), lo, hi, h)


def keep(x, out, sa, sb, l, h):
    for u in range(2):
        out[l, u] = x[u][EDGE : EDGE + COL]
        put_edges(sa, sb, (l, u), x[u][EDGE : 2 * EDGE], x[u][COL : COL + EDGE], h)


def gradient_kernel(wsum, vsum, ra, rb, states, gains, drifts, cn, cs, wide, out, sa, sb):
    h = half()
    for l in range(LV):
        n = [cn[l, u] for u in range(2)]
        s = [cs[l, u] for u in range(2)]
        x = None
        for k in reversed(range(STEPS)):
            m = []
            for u in range(2):
                left, right = get_edges(ra, rb, (k, l, u), h)
                w = jnp.concatenate([left, wsum[k, l, u], right], axis=0)
                v = jnp.concatenate(
                    [pltpu.roll(left, 4, 0), vsum[k, l, u], pltpu.roll(right, 4, 0)], axis=0
                )
                wide[k, l, u] = w
                m.append(v - w * states[k, l, u])
            x = m if x is None else [x[u] + m[u] for u in range(2)]
            x = adjoint(
                x, [gains[k, l, u] for u in range(2)], [drifts[k, l, u] for u in range(2)], n, s
            )
        keep(x, out, sa, sb, l, h)


def hessian(l, p, wide, gains, drifts, cn, cs):
    n = [cn[l, u] for u in range(2)]
    s = [cs[l, u] for u in range(2)]
    g = lambda k: [gains[k, l, u] for u in range(2)]
    d = lambda k: [drifts[k, l, u] for u in range(2)]
    e, seen = p, []
    for k in range(STEPS):
        e = tangent(e, g(k), d(k), n, s)
        seen.append([wide[k, l, u] * e[u] for u in range(2)])
    x = None
    for k in reversed(range(STEPS)):
        x = seen[k] if x is None else [x[u] + seen[k][u] for u in range(2)]
        x = adjoint(x, g(k), d(k), n, s)
    return [p[u] + x[u] for u in range(2)]


def extended(center, ra, rb, l, h):
    out = []
    for u in range(2):
        left, right = get_edges(ra, rb, (l, u), h)
        out.append(jnp.concatenate([left, center[l, u], right], axis=0))
    return out


def hessian_kernel(center, ra, rb, wide, gains, drifts, cn, cs, out, sa, sb):
    h = half()
    for l in range(LV):
        p = extended(center, ra, rb, l, h)
        keep(hessian(l, p, wide, gains, drifts, cn, cs), out, sa, sb, l, h)


def last_kernel(g, center, ra, rb, wide, gains, drifts, cn, cs, out):
    h = half()
    sums = [jnp.zeros((8, 128), F32) for _ in range(5)]

    def fold(a, b):
        prod = a * b
        return jnp.sum(prod.reshape(8, 8, 128), axis=0)

    for l in range(LV):
        p = extended(center, ra, rb, l, h)
        y = hessian(l, p, wide, gains, drifts, cn, cs)
        v = [
            [g[l, u] for u in range(2)],
            [center[l, u] for u in range(2)],
            [y[u][EDGE : EDGE + COL] for u in range(2)],
        ]
        for i, (a, b) in enumerate(((0, 0), (0, 1), (1, 1), (0, 2), (1, 2))):
            for u in range(2):
                sums[i] = sums[i] + fold(v[a][u], v[b][u])
        for i in range(3):
            t = jnp.concatenate(v[i], axis=0).T.reshape(LAT, 16, 128)
            out[:, i * 3 + l] = t
    row = sublanes((16, 128))
    table = jnp.zeros((16, 128), F32)
    for i in range(5):
        table = jnp.where(row == i, jnp.sum(sums[i], axis=0, keepdims=True), table)
    for b in range(LAT):
        out[b, 9] = table


def final_kernel(x, parts, increment, residual):
    total = jnp.sum(parts[...], axis=0)
    total = jnp.broadcast_to(jnp.sum(total, axis=1, keepdims=True), (8, 128))
    a00, a01, a11, a02, a12 = [total[i : i + 1] for i in range(5)]
    alpha = a00 / a01
    new = a00 - 2.0 * alpha * a01 + alpha * alpha * a11
    keep1 = 1.0 + new / a00
    curve = keep1 * (keep1 * a01 - alpha * (a02 + a11)) + alpha * alpha * a12
    second = new / curve
    a = alpha + second * keep1
    b = alpha * second
    low = lanes((16, 128)) < 64
    for level in range(12):
        q, l = level // 3, level % 3
        got = []
        for h in range(2):
            v0, v1, v2 = [x[2 * q + h, i * 3 + l] for i in range(3)]
            got.append((a * v0 - b * v1, v0 - a * v1 + b * v2))
        for i, ref in enumerate((increment, residual)):
            x0, x1 = got[0][i], got[1][i]
            ref[level, pl.ds(0, 16, stride=2), :] = jnp.where(low, x0, pltpu.roll(x1, 64, 1))
            ref[level, pl.ds(1, 16, stride=2), :] = jnp.where(low, pltpu.roll(x0, 64, 1), x1)


VM = pl.BlockSpec(memory_space=pltpu.VMEM)
SM = pl.BlockSpec(memory_space=pltpu.SMEM)


def call(kernel, outs, *args, scratch=(), scalars=0, flops=1000000):
    shapes = tuple(jax.ShapeDtypeStruct(s, F32) for s in outs)
    return pl.pallas_call(
        kernel,
        out_shape=shapes if len(shapes) > 1 else shapes[0],
        in_specs=[SM] * scalars + [VM] * (len(args) - scalars),
        out_specs=(VM,) * len(shapes) if len(shapes) > 1 else VM,
        scratch_shapes=list(scratch),
        name=kernel.__name__,
    )(*args)


def swap(sa, sb):
    near, far = [], []
    for i in range(LAT):
        for j in range(LON):
            me = i * LON + j
            near.append((me, (i ^ 1) * LON + j))
            other = (j + 1) % LON if i % 2 else (j - 1) % LON
            far.append((me, (i ^ 1) * LON + other))
    rb = lax.ppermute(sb, ("lat", "lon"), far)
    ra = lax.ppermute(sa, ("lat", "lon"), near)
    return ra, rb


def on_device(
    background, wind_lon, wind_lat, obs_value, obs_weight, obs_tile, obs_cell, obs_step, obs_count
):
    both = ("lat", "lon")
    plane = (LV, 2, EXT, 128)
    edge = (LV, 2, EDGE, 128)
    middle = (LV, 2, COL, 128)

    sent = call(prep_kernel, [(LAT, 9, 16, 128)], background, wind_lon, wind_lat)
    moved = lax.all_to_all(sent, "lat", 0, 0, tiled=True)
    fold = lambda a: a.reshape(16, 128)
    packed = call(
        pack_kernel,
        [(ALL, 8, 128)],
        obs_count,
        fold(obs_tile),
        fold(obs_cell),
        fold(obs_step),
        fold(obs_value),
        fold(obs_weight),
        scalars=1,
        scratch=[
            pltpu.VMEM((13, 16, 128), F32),
            pltpu.VMEM((128, 128), F32),
            pltpu.VMEM((128, 1024), F32),
            pltpu.VMEM((1024, 384), BF16),
        ],
    )
    fields, sa, sb = call(recv_kernel, [(9, 2, COL, 128)] + [(9, 2, EDGE, 128)] * 2, moved)
    ra, rb = swap(sa, sb)
    arrived = lax.all_to_all(packed, both, 0, 0, tiled=True)
    wsum, vsum, sa, sb = call(
        scatter_kernel,
        [(STEPS,) + middle] * 2 + [(STEPS,) + edge] * 2,
        arrived,
        scratch=[
            pltpu.VMEM((1024, 128), F32),
            pltpu.VMEM((ROWS, 1024), BF16),
            pltpu.VMEM((1280, 1024), BF16),
            pltpu.VMEM((ROWS, 1280), F32),
        ],
    )
    wa, wb = swap(sa, sb)
    states, gains, drifts, cn, cs = call(
        forward_kernel, [(STEPS,) + plane] * 3 + [plane] * 2, fields, ra, rb
    )
    wide, g, sa, sb = call(
        gradient_kernel,
        [(STEPS,) + plane, middle, edge, edge],
        wsum,
        vsum,
        wa,
        wb,
        states,
        gains,
        drifts,
        cn,
        cs,
    )
    ra, rb = swap(sa, sb)
    hg, sa, sb = call(
        hessian_kernel, [middle, edge, edge], g, ra, rb, wide, gains, drifts, cn, cs
    )
    ra, rb = swap(sa, sb)
    sent = call(
        last_kernel, [(LAT, 10, 16, 128)], g, hg, ra, rb, wide, gains, drifts, cn, cs
    )
    moved = lax.all_to_all(sent, "lat", 0, 0, tiled=True)
    mine = jnp.sum(moved[:, 9, :8], axis=0)
    parts = lax.all_to_all(
        jnp.broadcast_to(mine[None], (LON, 8, 128)), "lon", 0, 0, tiled=True
    )
    return call(final_kernel, [(12, 32, 128)] * 2, moved, parts)


def solution(mesh):
    grid = P(None, "lat", "lon")
    flat = P(("lat", "lon"))
    return jax.shard_map(
        on_device,
        mesh=mesh,
        in_specs=(grid, grid, grid, flat, flat, P(("lat", "lon"), None), flat, flat, flat),
        out_specs=(grid, grid),
        check_vma=False,
    )
```

```python
import jax
import jax.numpy as jnp
from jax import lax
from jax.experimental import pallas as pl
from jax.experimental.pallas import tpu as pltpu
from jax.sharding import PartitionSpec as P

LAT = 8
LON = 16
ALL = 128
STEPS = 4
LV = 3
COL = 64
EDGE = 8
EXT = COL + 2 * EDGE
ROOM = 256
ROWS = STEPS * LV * COL
F32 = jnp.float32
BF16 = jnp.bfloat16
I32 = jnp.int32


def lanes(shape):
    return lax.broadcasted_iota(I32, shape, len(shape) - 1)


def sublanes(shape):
    return lax.broadcasted_iota(I32, shape, len(shape) - 2)


def half():
    return lax.rem(lax.axis_index("lat"), 2)


def prep_kernel(bg, wl, wt, out):
    low = lanes((16, 128)) < 64
    for f, ref in enumerate((bg, wl, wt)):
        for level in range(12):
            q, l = level // 3, level % 3
            even = ref[level, pl.ds(0, 16, stride=2), :]
            odd = ref[level, pl.ds(1, 16, stride=2), :]
            out[2 * q, f * 3 + l] = jnp.where(low, even, pltpu.roll(odd, 64, 1))
            out[2 * q + 1, f * 3 + l] = jnp.where(low, pltpu.roll(even, 64, 1), odd)


def put_edges(sa, sb, index, lo, hi, h):
    @pl.when(h == 0)
    def _():
        sa[index] = hi
        sb[index] = lo

    @pl.when(h != 0)
    def _():
        sa[index] = lo
        sb[index] = hi


def get_edges(ra, rb, index, h):
    a, b = ra[index], rb[index]
    first = jnp.full(a.shape, h, I32) == 0
    return jnp.where(first, b, a), jnp.where(first, a, b)


def recv_kernel(x, center, sa, sb):
    h = half()
    for f in range(9):
        t = x[:, f].reshape(128, 128).T
        for u in range(2):
            center[f, u] = t[u * 64 : u * 64 + 64]
            put_edges(sa, sb, (f, u), t[u * 64 : u * 64 + 8], t[u * 64 + 56 : u * 64 + 64], h)


def up(x):
    return pltpu.roll(x, EXT - 1, 0)


def down(x):
    return pltpu.roll(x, 1, 0)


def north(e, o):
    return pltpu.roll(o, 1, 1), e


def south(e, o):
    return o, pltpu.roll(e, 127, 1)


def forward_kernel(center, ra, rb, states, gains, drifts, cn, cs):
    h = half()
    lane = lanes((EXT, 128))

    def ext(f, u):
        left, right = get_edges(ra, rb, (f, u), h)
        return jnp.concatenate([left, center[f, u], right], axis=0)

    for l in range(LV):
        s = [ext(l, u) for u in range(2)]
        wl = [ext(3 + l, u) for u in range(2)]
        wt = [ext(6 + l, u) for u in range(2)]
        n = [0.08 + 0.5 * wt[u] for u in range(2)]
        d = [0.08 - 0.5 * wt[u] for u in range(2)]
        n[0] = jnp.where(lane == 0, 0.0, n[0])
        d[1] = jnp.where(lane == 127, 0.0, d[1])
        for u in range(2):
            cn[l, u] = n[u]
            cs[l, u] = d[u]
        for k in range(STEPS):
            no, so = north(*s), south(*s)
            new = []
            for u in range(2):
                hi, lo = up(s[u]), down(s[u])
                drift = 0.5 * wl[u] + 0.1 * s[u]
                gains[k, l, u] = 0.68 - 0.1 * (hi - lo)
                drifts[k, l, u] = drift
                new.append(
                    0.68 * s[u] + 0.08 * (hi + lo) - drift * (hi - lo) + n[u] * no[u] + d[u] * so[u]
                )
            s = new
            for u in range(2):
                states[k, l, u] = s[u]


def tangent(e, g, d, n, s):
    no, so = north(*e), south(*e)
    out = []
    for u in range(2):
        hi, lo = up(e[u]), down(e[u])
        out.append(g[u] * e[u] + 0.08 * (hi + lo) - d[u] * (hi - lo) + n[u] * no[u] + s[u] * so[u])
    return out


def adjoint(x, g, d, n, s):
    no = north(s[0] * x[0], s[1] * x[1])
    so = south(n[0] * x[0], n[1] * x[1])
    out = []
    for u in range(2):
        flow = d[u] * x[u]
        wide = 0.08 * x[u]
        out.append(g[u] * x[u] + up(wide + flow) + down(wide - flow) + no[u] + so[u])
    return out


def pack_kernel(count, tile, cell, step, value, weight, out, rows, base, acc, left, right):
    shape = (16, 128)
    live = sublanes(shape) * 128 + lanes(shape) < count[0]
    c, t = cell[...], tile[...]
    level = c >> 12
    q = (level >= 3).astype(I32) + (level >= 6).astype(I32) + (level >= 9).astype(I32)
    row = (c & 4095) >> 7
    col = c & 127
    lat = (t >> 4) * 32 + row
    dest = (2 * q + (col >> 6)) * LON + (t & 15)
    w = jnp.where(live, weight[...], 0.0)
    w0 = w.astype(BF16).astype(F32)
    w1 = (w - w0).astype(BF16).astype(F32)
    wv = (w0 + w1) * value[...]
    v0 = wv.astype(BF16).astype(F32)
    v1 = (wv - v0).astype(BF16).astype(F32)
    rows[0] = jnp.where(live, dest, -1).astype(F32)
    rows[1] = (((level - 3 * q) * 64 + (col & 63)) * 256).astype(F32)
    rows[2] = ((lat & 1) * 128 + (lat >> 1)).astype(F32)
    rows[3] = step[...].astype(F32)
    rows[4] = w0
    rows[5] = w1
    rows[6] = v0
    rows[7] = v1
    rows[8] = wv - v0 - v1
    base[...] = jnp.zeros_like(base)
    acc[...] = jnp.zeros_like(acc)
    square = (128, 256)
    before = ((sublanes(square) < lanes(square)) | (lanes(square) >= 128)).astype(F32).astype(BF16)
    ids = sublanes((128, 128)).astype(F32)
    places = sublanes((ROOM, 128)).astype(F32)

    def block(i, carry):
        for j in range(2):
            line = lambda n: rows[n, pl.ds(2 * i + j, 1), :]
            at = slice(j * 128, j * 128 + 128)
            mine = ids == line(0)
            member = jnp.where(mine, 1.0, 0.0)
            counted = jnp.dot(member.astype(BF16), before, preferred_element_type=F32)
            rank = jnp.sum(member * (counted[:, :128] + base[...]), axis=0, keepdims=True)
            base[...] += counted[:, 128:]
            right[:, at] = jnp.where(places == rank, 1.0, 0.0).astype(BF16)
            for p in range(8):
                left[p * 128 : p * 128 + 128, at] = jnp.where(mine, line(1 + p), 0.0).astype(BF16)
        acc[...] += lax.dot_general(
            left[...], right[...], (((1,), (1,)), ((), ())), preferred_element_type=F32
        )
        return carry

    lax.fori_loop(0, 8, block, 0)
    for ch, pieces in enumerate(((0, 1), (2,), (3, 4), (5, 6, 7))):
        for hf in range(2):
            at = slice(hf * 128, hf * 128 + 128)
            out[:, 2 * ch + hf, :] = sum(acc[p * 128 : p * 128 + 128, at] for p in pieces)


def scatter_kernel(x, after, wsum, vsum, sa, sb, xt, at, bt, acc):
    h = half()
    most = jnp.max(x[:, 2:4, :], axis=0)
    total = jnp.sum(jnp.where(most > 0.5, 1.0, 0.0)).astype(I32)
    acc[...] = jnp.zeros_like(acc)
    for ch in range(4):
        xt[ch, :128] = x[:, 2 * ch, :].T

    @pl.when(total > 128)
    def _():
        for ch in range(4):
            xt[ch, 128:] = x[:, 2 * ch + 1, :].T

    row_ids = sublanes((ROWS, 128))
    lat_ids = sublanes((256, 128))

    def group(g, carry):
        def part(ch):
            return xt[ch, pl.ds(pl.multiple_of(g * 8, 8), 8), :]

        cell = part(0).astype(I32)
        row = (part(1).astype(I32) - 1) * (LV * COL) + (cell >> 8)
        lat = cell & 255
        w = part(2)
        v = part(3)
        w0 = w.astype(BF16).astype(F32)
        w1 = w - w0
        v0 = v.astype(BF16).astype(F32)
        v1 = (v - v0).astype(BF16).astype(F32)
        v2 = v - v0 - v1
        for r in range(8):
            cols = slice(r * 128, r * 128 + 128)
            at[:, cols] = jnp.where(row_ids == row[r : r + 1], 1.0, 0.0).astype(BF16)
            here = lat_ids == lat[r : r + 1]
            for p, piece in enumerate((w0, w1, v0, v1, v2)):
                bt[p * 256 : p * 256 + 256, cols] = jnp.where(here, piece[r : r + 1], 0.0).astype(BF16)
        acc[...] += lax.dot_general(
            at[...], bt[...], (((1,), (1,)), ((), ())), preferred_element_type=F32
        )
        return carry

    lax.fori_loop(0, (total + 7) // 8, group, 0)
    low = sublanes((8, 128)) < 4
    for k in range(STEPS):
        for l in range(LV):
            for u in range(2):
                rows = slice((k * LV + l) * COL, (k * LV + l + 1) * COL)
                take = lambda p: acc[rows, p * 256 + u * 128 : p * 256 + u * 128 + 128]
                w = take(0) + take(1)
                v = take(2) + take(3) + take(4)
                wsum[k, l, u] = w
                vsum[k, l, u] = v
                lo = jnp.where(low, w[:8], pltpu.roll(v[:8], 4, 0))
                hi = jnp.where(low, pltpu.roll(v[56:], 4, 0), w[56:])
                put_edges(sa, sb, (k, l, u), lo, hi, h)


def keep(x, out, sa, sb, l, h):
    for u in range(2):
        out[l, u] = x[u][EDGE : EDGE + COL]
        put_edges(sa, sb, (l, u), x[u][EDGE : 2 * EDGE], x[u][COL : COL + EDGE], h)


def fetch(sources, buffers, sems):
    levels = []
    for l in range(LV):
        copies = []
        for i, (src, dst) in enumerate(zip(sources, buffers)):
            at = (slice(None), l) if len(src.shape) == 5 else l
            copies.append(pltpu.make_async_copy(src.at[at], dst.at[at], sems.at[l, i]))
        levels.append(copies)
        for copy in copies:
            copy.start()
    return levels


def gradient_kernel(
    wsum, vsum, ra, rb, states_in, gains_in, drifts_in, cn_in, cs_in, out, sa, sb, *scratch
):
    *buffers, sems = scratch
    h = half()
    levels = fetch((states_in, gains_in, drifts_in, cn_in, cs_in), buffers, sems)
    states, gains, drifts, cn, cs = buffers
    for l in range(LV):
        for copy in levels[l]:
            copy.wait()
        n = [cn[l, u] for u in range(2)]
        s = [cs[l, u] for u in range(2)]
        x = None
        for k in reversed(range(STEPS)):
            m = []
            for u in range(2):
                left, right = get_edges(ra, rb, (k, l, u), h)
                w = jnp.concatenate([left, wsum[k, l, u], right], axis=0)
                v = jnp.concatenate(
                    [pltpu.roll(left, 4, 0), vsum[k, l, u], pltpu.roll(right, 4, 0)], axis=0
                )
                m.append(v - w * states[k, l, u])
            x = m if x is None else [x[u] + m[u] for u in range(2)]
            x = adjoint(
                x, [gains[k, l, u] for u in range(2)], [drifts[k, l, u] for u in range(2)], n, s
            )
        keep(x, out, sa, sb, l, h)


def hessian(l, p, wide, gains, drifts, cn, cs):
    n = [cn[l, u] for u in range(2)]
    s = [cs[l, u] for u in range(2)]
    g = lambda k: [gains[k, l, u] for u in range(2)]
    d = lambda k: [drifts[k, l, u] for u in range(2)]
    e, seen = p, []
    for k in range(STEPS):
        e = tangent(e, g(k), d(k), n, s)
        w = wide(k)
        seen.append([w[u] * e[u] for u in range(2)])
    x = None
    for k in reversed(range(STEPS)):
        x = seen[k] if x is None else [x[u] + seen[k][u] for u in range(2)]
        x = adjoint(x, g(k), d(k), n, s)
    return [p[u] + x[u] for u in range(2)]


def extended(center, ra, rb, index, h):
    out = []
    for u in range(2):
        left, right = get_edges(ra, rb, index + (u,), h)
        out.append(jnp.concatenate([left, center[index + (u,)], right], axis=0))
    return out


def hessian_kernel(
    center, ra, rb, wsum, wa, wb, gains_in, drifts_in, cn_in, cs_in, out, sa, sb, *scratch
):
    *buffers, sems = scratch
    h = half()
    levels = fetch((gains_in, drifts_in, cn_in, cs_in), buffers, sems)
    for l in range(LV):
        p = extended(center, ra, rb, (l,), h)
        for copy in levels[l]:
            copy.wait()
        wide = lambda k: extended(wsum, wa, wb, (k, l), h)
        keep(hessian(l, p, wide, *buffers), out, sa, sb, l, h)


def last_kernel(
    g, center, ra, rb, wsum, wa, wb, gains_in, drifts_in, cn_in, cs_in, out, table_ref, *scratch
):
    *buffers, sems = scratch
    h = half()
    levels = fetch((gains_in, drifts_in, cn_in, cs_in), buffers, sems)
    sums = [jnp.zeros((8, 128), F32) for _ in range(5)]

    def fold(a, b):
        prod = a * b
        return jnp.sum(prod.reshape(8, 8, 128), axis=0)

    for l in range(LV):
        p = extended(center, ra, rb, (l,), h)
        for copy in levels[l]:
            copy.wait()
        wide = lambda k: extended(wsum, wa, wb, (k, l), h)
        y = hessian(l, p, wide, *buffers)
        v = [
            [g[l, u] for u in range(2)],
            [center[l, u] for u in range(2)],
            [y[u][EDGE : EDGE + COL] for u in range(2)],
        ]
        for i, (a, b) in enumerate(((0, 0), (0, 1), (1, 1), (0, 2), (1, 2))):
            for u in range(2):
                sums[i] = sums[i] + fold(v[a][u], v[b][u])
        for i in range(3):
            t = jnp.concatenate(v[i], axis=0).T.reshape(LAT, 16, 128)
            out[:, i * 3 + l] = t
    lane = lanes((1, 128))
    table = jnp.zeros((1, 128), F32)
    for i in range(5):
        whole = jnp.sum(jnp.sum(sums[i], axis=0, keepdims=True), axis=1, keepdims=True)
        table = jnp.where(lane == i, whole, table)
    table_ref[...] = jnp.broadcast_to(table, (ALL, 128))


def final_kernel(x, parts, increment, residual):
    total = jnp.sum(parts[...], axis=0, keepdims=True)
    lane = lanes((1, 128))
    pick = lambda i: jnp.sum(jnp.where(lane == i, total, 0.0), axis=1, keepdims=True)
    a00, a01, a11, a02, a12 = [jnp.broadcast_to(pick(i), (1, 128)) for i in range(5)]
    alpha = a00 / a01
    new = a00 - 2.0 * alpha * a01 + alpha * alpha * a11
    keep1 = 1.0 + new / a00
    curve = keep1 * (keep1 * a01 - alpha * (a02 + a11)) + alpha * alpha * a12
    second = new / curve
    a = alpha + second * keep1
    b = alpha * second
    low = lanes((16, 128)) < 64
    for level in range(12):
        q, l = level // 3, level % 3
        got = []
        for h in range(2):
            v0, v1, v2 = [x[2 * q + h, i * 3 + l] for i in range(3)]
            got.append((a * v0 - b * v1, v0 - a * v1 + b * v2))
        for i, ref in enumerate((increment, residual)):
            x0, x1 = got[0][i], got[1][i]
            ref[level, pl.ds(0, 16, stride=2), :] = jnp.where(low, x0, pltpu.roll(x1, 64, 1))
            ref[level, pl.ds(1, 16, stride=2), :] = jnp.where(low, pltpu.roll(x0, 64, 1), x1)


VM = pl.BlockSpec(memory_space=pltpu.VMEM)
SM = pl.BlockSpec(memory_space=pltpu.SMEM)
AN = pl.BlockSpec(memory_space=pl.ANY)


def call(kernel, outs, *args, scratch=(), space="v", ins=None):
    shapes = tuple(
        pltpu.VMEM(s, F32) if where == "v" else jax.ShapeDtypeStruct(s, F32)
        for s, where in zip(outs, space * len(outs) if len(space) == 1 else space)
    )
    ins = ins or "v" * len(args)
    args = [
        pltpu.with_memory_space_constraint(a, pltpu.VMEM) if i == "v" else a
        for a, i in zip(args, ins)
    ]
    return pl.pallas_call(
        kernel,
        out_shape=shapes if len(shapes) > 1 else shapes[0],
        in_specs=[{"s": SM, "a": AN}.get(i, VM) for i in ins],
        out_specs=(VM,) * len(shapes) if len(shapes) > 1 else VM,
        scratch_shapes=list(scratch),
        name=kernel.__name__,
    )(*args)


def swap(sa, sb):
    near, far = [], []
    for i in range(LAT):
        for j in range(LON):
            me = i * LON + j
            near.append((me, (i ^ 1) * LON + j))
            other = (j + 1) % LON if i % 2 else (j - 1) % LON
            far.append((me, (i ^ 1) * LON + other))
    rb = lax.ppermute(sb, ("lat", "lon"), far)
    ra = lax.ppermute(sa, ("lat", "lon"), near)
    return ra, rb


def on_device(
    background, wind_lon, wind_lat, obs_value, obs_weight, obs_tile, obs_cell, obs_step, obs_count
):
    both = ("lat", "lon")
    plane = (LV, 2, EXT, 128)
    edge = (LV, 2, EDGE, 128)
    middle = (LV, 2, COL, 128)

    sent = call(
        prep_kernel, [(LAT, 9, 16, 128)], background, wind_lon, wind_lat, ins="hhh"
    )
    moved = lax.all_to_all(sent, "lat", 0, 0, tiled=True)
    fold = lambda a: a.reshape(16, 128)
    packed = call(
        pack_kernel,
        [(ALL, 8, 128)],
        obs_count,
        fold(obs_tile),
        fold(obs_cell),
        fold(obs_step),
        fold(obs_value),
        fold(obs_weight),
        ins="shhhhh",
        scratch=[
            pltpu.VMEM((9, 16, 128), F32),
            pltpu.VMEM((128, 128), F32),
            pltpu.VMEM((1024, 256), F32),
            pltpu.VMEM((1024, 256), BF16),
            pltpu.VMEM((256, 256), BF16),
        ],
    )
    moved, packed = lax.optimization_barrier((moved, packed))
    arrived = lax.all_to_all(packed, both, 0, 0, tiled=True)
    fields, sa, sb = call(recv_kernel, [(9, 2, COL, 128)] + [(9, 2, EDGE, 128)] * 2, moved)
    ra, rb = swap(sa, sb)
    states, gains, drifts, cn, cs = call(
        forward_kernel, [(STEPS,) + plane] * 3 + [plane] * 2, fields, ra, rb, space="h"
    )
    wsum, vsum, sa, sb = call(
        scatter_kernel,
        [(STEPS,) + middle] * 2 + [(STEPS,) + edge] * 2,
        arrived,
        cn,
        ins="va",
        scratch=[
            pltpu.VMEM((4, 256, 128), F32),
            pltpu.VMEM((ROWS, 1024), BF16),
            pltpu.VMEM((1280, 1024), BF16),
            pltpu.VMEM((ROWS, 1280), F32),
        ],
    )
    wa, wb = swap(sa, sb)
    big = pltpu.VMEM((STEPS,) + plane, F32)
    small = pltpu.VMEM(plane, F32)
    sems = lambda n: pltpu.SemaphoreType.DMA((LV, n))
    g, sa, sb = call(
        gradient_kernel,
        [middle, edge, edge],
        wsum,
        vsum,
        wa,
        wb,
        states,
        gains,
        drifts,
        cn,
        cs,
        ins="vvvvaaaaa",
        scratch=[big, big, big, small, small, sems(5)],
    )
    ra, rb = swap(sa, sb)
    coefs = (wsum, wa, wb, gains, drifts, cn, cs)
    scratch = [big, big, small, small, sems(4)]
    hg, sa, sb = call(
        hessian_kernel, [middle, edge, edge], g, ra, rb, *coefs, ins="vvvvvvaaaa", scratch=scratch
    )
    ra, rb = swap(sa, sb)
    sent, table = call(
        last_kernel,
        [(LAT, 9, 16, 128), (ALL, 128)],
        g,
        hg,
        ra,
        rb,
        *coefs,
        ins="vvvvvvvaaaa",
        scratch=scratch,
    )
    parts = lax.all_to_all(table, both, 0, 0, tiled=True)
    moved = lax.all_to_all(sent, "lat", 0, 0, tiled=True)
    return call(final_kernel, [(12, 32, 128)] * 2, moved, parts, space="h")


def solution(mesh):
    grid = P(None, "lat", "lon")
    flat = P(("lat", "lon"))
    return jax.shard_map(
        on_device,
        mesh=mesh,
        in_specs=(grid, grid, grid, flat, flat, P(("lat", "lon"), None), flat, flat, flat),
        out_specs=(grid, grid),
        check_vma=False,
    )
```

```python
import jax
import jax.numpy as jnp
from jax import lax
from jax.experimental import pallas as pl
from jax.experimental.pallas import tpu as pltpu
from jax.sharding import PartitionSpec as P


LAT = 8
LON = 16
ALL = 128
STEPS = 4
LV = 3
COL = 64
EDGE = 24
EXT = COL + 2 * EDGE
SLAB = 40
ROOM = 256
ROWS = STEPS * LV * COL
F32 = jnp.float32
BF16 = jnp.bfloat16
I32 = jnp.int32


def lanes(shape):
    return lax.broadcasted_iota(I32, shape, len(shape) - 1)


def sublanes(shape):
    return lax.broadcasted_iota(I32, shape, len(shape) - 2)


def half():
    return lax.rem(lax.axis_index("lat"), 2)


def prep_kernel(bg, wl, wt, out):
    low = lanes((16, 128)) < 64
    for f, ref in enumerate((bg, wl, wt)):
        for level in range(12):
            q, l = level // 3, level % 3
            even = ref[level, pl.ds(0, 16, stride=2), :]
            odd = ref[level, pl.ds(1, 16, stride=2), :]
            out[2 * q, f * 3 + l] = jnp.where(low, even, pltpu.roll(odd, 64, 1))
            out[2 * q + 1, f * 3 + l] = jnp.where(low, pltpu.roll(even, 64, 1), odd)


def put_edges(sa, sb, index, lo, hi, h):
    @pl.when(h == 0)
    def _():
        sa[index] = hi
        sb[index] = lo

    @pl.when(h != 0)
    def _():
        sa[index] = lo
        sb[index] = hi


def get_edges(ra, rb, index, h):
    a, b = ra[index], rb[index]
    first = jnp.full(a.shape, h, I32) == 0
    return jnp.where(first, b, a), jnp.where(first, a, b)


def recv_kernel(x, center, sa, sb):
    h = half()
    for f in range(9):
        t = x[:, f].reshape(128, 128).T
        for u in range(2):
            center[f, u] = t[u * 64 : u * 64 + 64]
            lo = t[u * 64 : u * 64 + EDGE]
            hi = t[u * 64 + COL - EDGE : u * 64 + COL]
            put_edges(sa, sb, (f, u), lo, hi, h)


def up(x):
    return pltpu.roll(x, x.shape[0] - 1, 0)


def down(x):
    return pltpu.roll(x, 1, 0)


def north(e, o):
    return pltpu.roll(o, 1, 1), e


def south(e, o):
    return o, pltpu.roll(e, 127, 1)


def forward_kernel(center, ra, rb, states, gains, drifts, cn, cs):
    h = half()
    lane = lanes((EXT, 128))

    def ext(f, u):
        left, right = get_edges(ra, rb, (f, u), h)
        return jnp.concatenate([left, center[f, u], right], axis=0)

    for l in range(LV):
        s = [ext(l, u) for u in range(2)]
        wl = [ext(3 + l, u) for u in range(2)]
        wt = [ext(6 + l, u) for u in range(2)]
        n = [0.08 + 0.5 * wt[u] for u in range(2)]
        d = [0.08 - 0.5 * wt[u] for u in range(2)]
        n[0] = jnp.where(lane == 0, 0.0, n[0])
        d[1] = jnp.where(lane == 127, 0.0, d[1])
        for u in range(2):
            cn[l, u] = n[u]
            cs[l, u] = d[u]
        for k in range(STEPS):
            no, so = north(*s), south(*s)
            new = []
            for u in range(2):
                hi, lo = up(s[u]), down(s[u])
                drift = 0.5 * wl[u] + 0.1 * s[u]
                gains[k, l, u] = 0.68 - 0.1 * (hi - lo)
                drifts[k, l, u] = drift
                new.append(
                    0.68 * s[u] + 0.08 * (hi + lo) - drift * (hi - lo) + n[u] * no[u] + d[u] * so[u]
                )
            s = new
            for u in range(2):
                states[k, l, u] = s[u]


def tangent(e, g, d, n, s):
    no, so = north(*e), south(*e)
    out = []
    for u in range(2):
        hi, lo = up(e[u]), down(e[u])
        out.append(g[u] * e[u] + 0.08 * (hi + lo) - d[u] * (hi - lo) + n[u] * no[u] + s[u] * so[u])
    return out


def adjoint(x, g, d, n, s):
    no = north(s[0] * x[0], s[1] * x[1])
    so = south(n[0] * x[0], n[1] * x[1])
    out = []
    for u in range(2):
        flow = d[u] * x[u]
        wide = 0.08 * x[u]
        out.append(g[u] * x[u] + up(wide + flow) + down(wide - flow) + no[u] + so[u])
    return out


def pack_kernel(count, tile, cell, step, value, weight, out, rows, member, counted, acc, left, right):
    shape = (16, 128)
    live = sublanes(shape) * 128 + lanes(shape) < count[0]
    c, t = cell[...], tile[...]
    level = c >> 12
    q = (level >= 3).astype(I32) + (level >= 6).astype(I32) + (level >= 9).astype(I32)
    row = (c & 4095) >> 7
    col = c & 127
    lat = (t >> 4) * 32 + row
    dest = (2 * q + (col >> 6)) * LON + (t & 15)
    w = jnp.where(live, weight[...], 0.0)
    w0 = w.astype(BF16).astype(F32)
    w1 = (w - w0).astype(BF16).astype(F32)
    wv = (w0 + w1) * value[...]
    v0 = wv.astype(BF16).astype(F32)
    v1 = (wv - v0).astype(BF16).astype(F32)
    rows[0] = jnp.where(live, dest, -1).astype(F32)
    rows[1] = (((level - 3 * q) * 64 + (col & 63)) * 256).astype(F32)
    rows[2] = ((lat & 1) * 128 + (lat >> 1)).astype(F32)
    rows[3] = step[...].astype(F32)
    rows[4] = w0
    rows[5] = w1
    rows[6] = v0
    rows[7] = v1
    rows[8] = wv - v0 - v1
    square = (128, 256)
    before = ((sublanes(square) < lanes(square)) | (lanes(square) >= 128)).astype(F32).astype(BF16)
    ids = sublanes((128, 128)).astype(F32)
    places = sublanes((ROOM, 128)).astype(F32)
    for b in range(16):
        at = slice(b * 128, b * 128 + 128)
        mine = ids == rows[0, b : b + 1, :]
        member[at, :] = jnp.where(mine, 1.0, 0.0).astype(BF16)
        for p in range(8):
            piece = rows[1 + p, b : b + 1, :]
            left[p * 128 : p * 128 + 128, at] = jnp.where(mine, piece, 0.0).astype(BF16)
    counted[...] = jnp.dot(member[...], before, preferred_element_type=F32)
    base = jnp.zeros((128, 128), F32)
    for b in range(16):
        at = slice(b * 128, b * 128 + 128)
        mine = ids == rows[0, b : b + 1, :]
        rank = jnp.where(mine, counted[at, :128] + base, 0.0)
        rank = jnp.sum(rank, axis=0, keepdims=True)
        base = base + counted[at, 128:]
        right[:, at] = jnp.where(places == rank, 1.0, 0.0).astype(BF16)
    acc[...] = lax.dot_general(
        left[...], right[...], (((1,), (1,)), ((), ())), preferred_element_type=F32
    )
    for ch, pieces in enumerate(((0, 1), (2,), (3, 4), (5, 6, 7))):
        for hf in range(2):
            at = slice(hf * 128, hf * 128 + 128)
            out[:, 2 * ch + hf, :] = sum(acc[p * 128 : p * 128 + 128, at] for p in pieces)


def scatter_kernel(x, wsum, vsum, sa, sb, xt, at, bt, acc):
    h = half()
    most = jnp.max(x[:, 2:4, :], axis=0)
    total = jnp.sum(jnp.where(most > 0.5, 1.0, 0.0)).astype(I32)
    acc[...] = jnp.zeros_like(acc)
    for ch in range(4):
        xt[ch, :128] = x[:, 2 * ch, :].T

    @pl.when(total > 128)
    def _():
        for ch in range(4):
            xt[ch, 128:] = x[:, 2 * ch + 1, :].T

    row_ids = sublanes((ROWS, 128))
    lat_ids = sublanes((256, 128))

    def group(g, carry):
        def part(ch):
            return xt[ch, pl.ds(pl.multiple_of(g * 8, 8), 8), :]

        cell = part(0).astype(I32)
        row = (part(1).astype(I32) - 1) * (LV * COL) + (cell >> 8)
        lat = cell & 255
        w = part(2)
        v = part(3)
        w0 = w.astype(BF16).astype(F32)
        w1 = w - w0
        v0 = v.astype(BF16).astype(F32)
        v1 = (v - v0).astype(BF16).astype(F32)
        v2 = v - v0 - v1
        for r in range(8):
            cols = slice(r * 128, r * 128 + 128)
            at[:, cols] = jnp.where(row_ids == row[r : r + 1], 1.0, 0.0).astype(BF16)
            here = lat_ids == lat[r : r + 1]
            for p, piece in enumerate((w0, w1, v0, v1, v2)):
                bt[p * 256 : p * 256 + 256, cols] = jnp.where(here, piece[r : r + 1], 0.0).astype(BF16)
        acc[...] += lax.dot_general(
            at[...], bt[...], (((1,), (1,)), ((), ())), preferred_element_type=F32
        )
        return carry

    lax.fori_loop(0, (total + 7) // 8, group, 0)
    low = sublanes((8, 128)) < 4
    for k in range(STEPS):
        for l in range(LV):
            for u in range(2):
                rows = slice((k * LV + l) * COL, (k * LV + l + 1) * COL)
                take = lambda p: acc[rows, p * 256 + u * 128 : p * 256 + u * 128 + 128]
                w = take(0) + take(1)
                v = take(2) + take(3) + take(4)
                wsum[k, l, u] = w
                vsum[k, l, u] = v
                mix = jnp.where(low, w[16:24], pltpu.roll(v[16:24], 4, 0))
                lo = jnp.concatenate([w[:16], v[:16], mix], axis=0)
                mix = jnp.where(low, pltpu.roll(v[40:48], 4, 0), w[40:48])
                hi = jnp.concatenate([w[48:], v[48:], mix], axis=0)
                put_edges(sa, sb, (k, l, u), lo, hi, h)


def fetch(sources, buffers, sems):
    levels = []
    for l in range(LV):
        copies = []
        for i, (src, dst) in enumerate(zip(sources, buffers)):
            at = (slice(None), l) if len(src.shape) == 5 else l
            copies.append(pltpu.make_async_copy(src.at[at], dst.at[at], sems.at[l, i]))
        levels.append(copies)
        for copy in copies:
            copy.start()
    return levels


def hessian(p, wide, gains, drifts, n, s):
    e, seen = p, []
    for k in range(STEPS):
        e = tangent(e, gains(k), drifts(k), n, s)
        w = wide(k)
        seen.append([w[u] * e[u] for u in range(2)])
    x = None
    for k in reversed(range(STEPS)):
        x = seen[k] if x is None else [x[u] + seen[k][u] for u in range(2)]
        x = adjoint(x, gains(k), drifts(k), n, s)
    return [p[u] + x[u] for u in range(2)]


def core_kernel(
    ra, rb, w_in, v_in, states_in, gains_in, drifts_in, cn_in, cs_in, out, *scratch
):
    *buffers, sems = scratch
    h = half()
    levels = fetch((w_in, v_in, states_in, gains_in, drifts_in, cn_in, cs_in), buffers, sems)
    wsum, vsum, states, gains, drifts, cn, cs = buffers
    sums = [jnp.zeros((8, 128), F32) for _ in range(5)]

    def fold(a, b):
        prod = a * b
        return jnp.sum(prod.reshape(8, 8, 128), axis=0)

    for l in range(LV):
        for copy in levels[l]:
            copy.wait()

        def window(ref, first):
            return lambda k: [ref[k, l, u, first : EXT - first] for u in range(2)]

        def still(ref, first):
            return [ref[l, u, first : EXT - first] for u in range(2)]

        def weights(first):
            def at(k):
                got = []
                for u in range(2):
                    left, right = get_edges(ra, rb, (k, l, u), h)
                    skip = first - 8
                    got.append(
                        jnp.concatenate(
                            [left[skip:16], wsum[k, l, u], right[: 16 - skip]], axis=0
                        )
                    )
                return got

            return at

        n, s = still(cn, 0), still(cs, 0)
        x = None
        for k in reversed(range(STEPS)):
            m = []
            for u in range(2):
                left, right = get_edges(ra, rb, (k, l, u), h)
                lm, rm = left[32:], right[32:]
                w = jnp.concatenate([lm, left[:16], wsum[k, l, u], right[:16], rm], axis=0)
                lm, rm = pltpu.roll(lm, 4, 0), pltpu.roll(rm, 4, 0)
                v = jnp.concatenate([lm, left[16:32], vsum[k, l, u], right[16:32], rm], axis=0)
                m.append(v - w * states[k, l, u])
            x = m if x is None else [x[u] + m[u] for u in range(2)]
            x = adjoint(x, window(gains, 0)(k), window(drifts, 0)(k), n, s)
        vectors = [x]
        for first in (8, 16):
            p = [x[u][8 : x[u].shape[0] - 8] for u in range(2)]
            x = hessian(
                p,
                weights(first),
                window(gains, first),
                window(drifts, first),
                still(cn, first),
                still(cs, first),
            )
            vectors.append(x)
        v = [
            [y[u][edge : edge + COL] for u in range(2)] for y, edge in zip(vectors, (24, 16, 8))
        ]
        for i, (a, b) in enumerate(((0, 0), (0, 1), (1, 1), (0, 2), (1, 2))):
            for u in range(2):
                sums[i] = sums[i] + fold(v[a][u], v[b][u])
        for i in range(3):
            t = jnp.concatenate(v[i], axis=0).T
            for b in range(LAT):
                first = (i * 3 + l) * 16
                out[b, first : first + 16] = t[b * 16 : b * 16 + 16]
    lane = lanes((1, 128))
    table = jnp.zeros((1, 128), F32)
    for i in range(5):
        whole = jnp.sum(jnp.sum(sums[i], axis=0, keepdims=True), axis=1, keepdims=True)
        table = jnp.where(lane == i, whole, table)
    for b in range(LAT):
        out[b, 144:] = jnp.broadcast_to(table, (8, 128))


def share_kernel(x, out):
    total = jnp.sum(x[:, 144:152], axis=0)
    for j in range(LON):
        out[j] = total


def final_kernel(x, parts, increment, residual):
    total = jnp.sum(parts[...], axis=0)[:1]
    lane = lanes((1, 128))
    pick = lambda i: jnp.sum(jnp.where(lane == i, total, 0.0), axis=1, keepdims=True)
    a00, a01, a11, a02, a12 = [jnp.broadcast_to(pick(i), (1, 128)) for i in range(5)]
    alpha = a00 / a01
    new = a00 - 2.0 * alpha * a01 + alpha * alpha * a11
    keep1 = 1.0 + new / a00
    curve = keep1 * (keep1 * a01 - alpha * (a02 + a11)) + alpha * alpha * a12
    second = new / curve
    a = alpha + second * keep1
    b = alpha * second
    low = lanes((16, 128)) < 64
    for level in range(12):
        q, l = level // 3, level % 3
        got = []
        for h in range(2):
            v0, v1, v2 = [
                x[2 * q + h, (i * 3 + l) * 16 : (i * 3 + l) * 16 + 16] for i in range(3)
            ]
            got.append((a * v0 - b * v1, v0 - a * v1 + b * v2))
        for i, ref in enumerate((increment, residual)):
            x0, x1 = got[0][i], got[1][i]
            ref[level, pl.ds(0, 16, stride=2), :] = jnp.where(low, x0, pltpu.roll(x1, 64, 1))
            ref[level, pl.ds(1, 16, stride=2), :] = jnp.where(low, pltpu.roll(x0, 64, 1), x1)


VM = pl.BlockSpec(memory_space=pltpu.VMEM)
SM = pl.BlockSpec(memory_space=pltpu.SMEM)
AN = pl.BlockSpec(memory_space=pl.ANY)


def call(kernel, outs, *args, scratch=(), space="v", ins=None):
    shapes = tuple(
        pltpu.VMEM(s, F32) if where == "v" else jax.ShapeDtypeStruct(s, F32)
        for s, where in zip(outs, space * len(outs) if len(space) == 1 else space)
    )
    ins = ins or "v" * len(args)
    args = [
        pltpu.with_memory_space_constraint(a, pltpu.VMEM) if i == "v" else a
        for a, i in zip(args, ins)
    ]
    return make(kernel, shapes, ins, scratch)(*args)


def make(kernel, shapes, ins, scratch):
    return pl.pallas_call(
        kernel,
        out_shape=shapes if len(shapes) > 1 else shapes[0],
        in_specs=[{"s": SM, "a": AN}.get(i, VM) for i in ins],
        out_specs=(VM,) * len(shapes) if len(shapes) > 1 else VM,
        scratch_shapes=list(scratch),
    )


def swap(sa, sb):
    near, far = [], []
    for i in range(LAT):
        for j in range(LON):
            me = i * LON + j
            near.append((me, (i ^ 1) * LON + j))
            other = (j + 1) % LON if i % 2 else (j - 1) % LON
            far.append((me, (i ^ 1) * LON + other))
    rb = lax.ppermute(sb, ("lat", "lon"), far)
    ra = lax.ppermute(sa, ("lat", "lon"), near)
    return ra, rb


def on_device(
    background, wind_lon, wind_lat, obs_value, obs_weight, obs_tile, obs_cell, obs_step, obs_count
):
    both = ("lat", "lon")
    plane = (LV, 2, EXT, 128)
    middle = (LV, 2, COL, 128)

    fold = lambda a: a.reshape(16, 128)
    packed = call(
        pack_kernel,
        [(ALL, 8, 128)],
        obs_count,
        fold(obs_tile),
        fold(obs_cell),
        fold(obs_step),
        fold(obs_value),
        fold(obs_weight),
        ins="shhhhh",
        scratch=[
            pltpu.VMEM((9, 16, 128), F32),
            pltpu.VMEM((2048, 128), BF16),
            pltpu.VMEM((2048, 256), F32),
            pltpu.VMEM((1024, 256), F32),
            pltpu.VMEM((1024, 2048), BF16),
            pltpu.VMEM((256, 2048), BF16),
        ],
    )
    arrived = lax.all_to_all(packed, both, 0, 0, tiled=True)
    sent = call(prep_kernel, [(LAT, 9, 16, 128)], background, wind_lon, wind_lat, ins="hhh")
    moved = lax.all_to_all(sent, "lat", 0, 0, tiled=True)
    fields, sa, sb = call(
        recv_kernel,
        [(9, 2, COL, 128)] + [(9, 2, EDGE, 128)] * 2,
        moved,
        space="hvv",
    )
    ra, rb = swap(sa, sb)
    wsum, vsum, sa, sb = call(
        scatter_kernel,
        [(STEPS,) + middle] * 2 + [(STEPS, LV, 2, SLAB, 128)] * 2,
        arrived,
        space="hhvv",
        scratch=[
            pltpu.VMEM((4, 256, 128), F32),
            pltpu.VMEM((ROWS, 1024), BF16),
            pltpu.VMEM((1280, 1024), BF16),
            pltpu.VMEM((ROWS, 1280), F32),
        ],
    )
    wa, wb = swap(sa, sb)
    coefs = call(
        forward_kernel, [(STEPS,) + plane] * 3 + [plane] * 2, fields, ra, rb, ins="hvv", space="h"
    )
    big = pltpu.VMEM((STEPS,) + plane, F32)
    mid = pltpu.VMEM((STEPS,) + middle, F32)
    small = pltpu.VMEM(plane, F32)
    sent = call(
        core_kernel,
        [(LAT, 152, 128)],
        wa,
        wb,
        wsum,
        vsum,
        *coefs,
        ins="vv" + "a" * 7,
        scratch=[mid, mid, big, big, big, small, small, pltpu.SemaphoreType.DMA((LV, 7))],
    )
    moved = lax.all_to_all(sent, "lat", 0, 0, tiled=True)
    parts = lax.all_to_all(call(share_kernel, [(LON, 8, 128)], moved), "lon", 0, 0, tiled=True)
    return call(final_kernel, [(12, 32, 128)] * 2, moved, parts, space="h")


def solution(mesh):
    grid = P(None, "lat", "lon")
    flat = P(("lat", "lon"))

    return jax.shard_map(
        on_device,
        mesh=mesh,
        in_specs=(grid, grid, grid, flat, flat, P(("lat", "lon"), None), flat, flat, flat),
        out_specs=(grid, grid),
        check_vma=False,
    )
```

```python
import jax
import jax.numpy as jnp
from jax import lax
from jax.experimental import pallas as pl
from jax.experimental.pallas import tpu as pltpu
from jax.sharding import PartitionSpec as P


LAT = 8
LON = 16
ALL = 128
STEPS = 4
LV = 3
COL = 64
EDGE = 24
EXT = COL + 2 * EDGE
SLAB = 40
ROOM = 256
ROWS = STEPS * LV * COL
F32 = jnp.float32
BF16 = jnp.bfloat16
I32 = jnp.int32


def lanes(shape):
    return lax.broadcasted_iota(I32, shape, len(shape) - 1)


def sublanes(shape):
    return lax.broadcasted_iota(I32, shape, len(shape) - 2)


def half():
    return lax.rem(lax.axis_index("lat"), 2)


def prep_kernel(bg, wl, wt, *outs):
    low = lanes((16, 128)) < 64
    me = lax.axis_index("lat")
    for m, out in enumerate(outs):
        dest = me ^ m
        q, h = dest >> 1, dest & 1
        for f, ref in enumerate((bg, wl, wt)):
            for l in range(LV):
                even = ref[3 * q + l, pl.ds(0, 16, stride=2), :]
                odd = ref[3 * q + l, pl.ds(1, 16, stride=2), :]
                even = pltpu.roll(even, 64 * h, 1)
                odd = pltpu.roll(odd, 64 - 64 * h, 1)
                out[f * 3 + l] = jnp.where(low, even, odd)


def put_edges(sa, sb, index, lo, hi, h):
    @pl.when(h == 0)
    def _():
        sa[index] = hi
        sb[index] = lo

    @pl.when(h != 0)
    def _():
        sa[index] = lo
        sb[index] = hi


def get_edges(ra, rb, index, h):
    a, b = ra[index], rb[index]
    first = jnp.full(a.shape, h, I32) == 0
    return jnp.where(first, b, a), jnp.where(first, a, b)


def recv_kernel(*refs):
    *xs, center, sa, sb, buf = refs
    h = half()
    me = lax.axis_index("lat")
    for m, x in enumerate(xs):
        at = pl.ds(pl.multiple_of((me ^ m) * 16, 16), 16)
        for f in range(9):
            buf[f, at, :] = x[f]
    for f in range(9):
        t = buf[f].T
        for u in range(2):
            center[f, u] = t[u * 64 : u * 64 + 64]
            lo = t[u * 64 : u * 64 + EDGE]
            hi = t[u * 64 + COL - EDGE : u * 64 + COL]
            put_edges(sa, sb, (f, u), lo, hi, h)


def up(x):
    return pltpu.roll(x, x.shape[0] - 1, 0)


def down(x):
    return pltpu.roll(x, 1, 0)


def north(e, o):
    return pltpu.roll(o, 1, 1), e


def south(e, o):
    return o, pltpu.roll(e, 127, 1)


def forward_kernel(center, ra, rb, states, gains, drifts, cn, cs):
    h = half()
    lane = lanes((EXT, 128))

    def ext(f, u):
        left, right = get_edges(ra, rb, (f, u), h)
        return jnp.concatenate([left, center[f, u], right], axis=0)

    for l in range(LV):
        s = [ext(l, u) for u in range(2)]
        wl = [ext(3 + l, u) for u in range(2)]
        wt = [ext(6 + l, u) for u in range(2)]
        n = [0.08 + 0.5 * wt[u] for u in range(2)]
        d = [0.08 - 0.5 * wt[u] for u in range(2)]
        n[0] = jnp.where(lane == 0, 0.0, n[0])
        d[1] = jnp.where(lane == 127, 0.0, d[1])
        for u in range(2):
            cn[l, u] = n[u]
            cs[l, u] = d[u]
        for k in range(STEPS):
            no, so = north(*s), south(*s)
            new = []
            for u in range(2):
                hi, lo = up(s[u]), down(s[u])
                drift = 0.5 * wl[u] + 0.1 * s[u]
                gains[k, l, u] = 0.68 - 0.1 * (hi - lo)
                drifts[k, l, u] = drift
                new.append(
                    0.68 * s[u] + 0.08 * (hi + lo) - drift * (hi - lo) + n[u] * no[u] + d[u] * so[u]
                )
            s = new
            for u in range(2):
                states[k, l, u] = s[u]


def tangent(e, g, d, n, s):
    no, so = north(*e), south(*e)
    out = []
    for u in range(2):
        hi, lo = up(e[u]), down(e[u])
        out.append(g[u] * e[u] + 0.08 * (hi + lo) - d[u] * (hi - lo) + n[u] * no[u] + s[u] * so[u])
    return out


def adjoint(x, g, d, n, s):
    no = north(s[0] * x[0], s[1] * x[1])
    so = south(n[0] * x[0], n[1] * x[1])
    out = []
    for u in range(2):
        flow = d[u] * x[u]
        wide = 0.08 * x[u]
        out.append(g[u] * x[u] + up(wide + flow) + down(wide - flow) + no[u] + so[u])
    return out


def pack_kernel(count, tile, cell, step, value, weight, out, rows, member, counted, acc, left, right):
    shape = (16, 128)
    live = sublanes(shape) * 128 + lanes(shape) < count[0]
    c, t = cell[...], tile[...]
    level = c >> 12
    q = (level >= 3).astype(I32) + (level >= 6).astype(I32) + (level >= 9).astype(I32)
    row = (c & 4095) >> 7
    col = c & 127
    lat = (t >> 4) * 32 + row
    dest = (2 * q + (col >> 6)) * LON + (t & 15)
    w = jnp.where(live, weight[...], 0.0)
    w0 = w.astype(BF16).astype(F32)
    w1 = (w - w0).astype(BF16).astype(F32)
    wv = (w0 + w1) * value[...]
    v0 = wv.astype(BF16).astype(F32)
    v1 = (wv - v0).astype(BF16).astype(F32)
    rows[0] = jnp.where(live, dest, -1).astype(F32)
    rows[1] = (((level - 3 * q) * 64 + (col & 63)) * 256).astype(F32)
    rows[2] = ((lat & 1) * 128 + (lat >> 1)).astype(F32)
    rows[3] = step[...].astype(F32)
    rows[4] = w0
    rows[5] = w1
    rows[6] = v0
    rows[7] = v1
    rows[8] = wv - v0 - v1
    square = (128, 256)
    before = ((sublanes(square) < lanes(square)) | (lanes(square) >= 128)).astype(F32).astype(BF16)
    ids = sublanes((128, 128)).astype(F32)
    places = sublanes((ROOM, 128)).astype(F32)
    for b in range(16):
        at = slice(b * 128, b * 128 + 128)
        mine = ids == rows[0, b : b + 1, :]
        member[at, :] = jnp.where(mine, 1.0, 0.0).astype(BF16)
        for p in range(8):
            piece = rows[1 + p, b : b + 1, :]
            left[p * 128 : p * 128 + 128, at] = jnp.where(mine, piece, 0.0).astype(BF16)
    counted[...] = jnp.dot(member[...], before, preferred_element_type=F32)
    base = jnp.zeros((128, 128), F32)
    for b in range(16):
        at = slice(b * 128, b * 128 + 128)
        mine = ids == rows[0, b : b + 1, :]
        rank = jnp.where(mine, counted[at, :128] + base, 0.0)
        rank = jnp.sum(rank, axis=0, keepdims=True)
        base = base + counted[at, 128:]
        right[:, at] = jnp.where(places == rank, 1.0, 0.0).astype(BF16)
    acc[...] = lax.dot_general(
        left[...], right[...], (((1,), (1,)), ((), ())), preferred_element_type=F32
    )
    for ch, pieces in enumerate(((0, 1), (2,), (3, 4), (5, 6, 7))):
        for hf in range(2):
            at = slice(hf * 128, hf * 128 + 128)
            out[:, 2 * ch + hf, :] = sum(acc[p * 128 : p * 128 + 128, at] for p in pieces)


def scatter_kernel(x, wsum, vsum, sa, sb, xt, at, bt, acc):
    h = half()
    most = jnp.max(x[:, 2:4, :], axis=0)
    total = jnp.sum(jnp.where(most > 0.5, 1.0, 0.0)).astype(I32)
    acc[...] = jnp.zeros_like(acc)
    for ch in range(4):
        xt[ch, :128] = x[:, 2 * ch, :].T

    @pl.when(total > 128)
    def _():
        for ch in range(4):
            xt[ch, 128:] = x[:, 2 * ch + 1, :].T

    row_ids = sublanes((LV * COL, 128))
    lat_ids = sublanes((256, 128))

    def group(g, carry):
        def part(ch):
            return xt[ch, pl.ds(pl.multiple_of(g * 8, 8), 8), :]

        cell = part(0).astype(I32)
        step = part(1).astype(I32)
        row = cell >> 8
        lat = cell & 255
        w = part(2)
        v = part(3)
        w0 = w.astype(BF16).astype(F32)
        w1 = w - w0
        v0 = v.astype(BF16).astype(F32)
        v1 = (v - v0).astype(BF16).astype(F32)
        v2 = v - v0 - v1
        for r in range(8):
            cols = slice(r * 128, r * 128 + 128)

            def line(x):
                return jnp.broadcast_to(x[r : r + 1], (16, 128)).astype(BF16)

            def times(hot, x):
                return (hot.reshape(-1, 16, 128) * line(x)[None]).reshape(-1, 128)

            hot = jnp.where(row_ids == row[r : r + 1], 1.0, 0.0).astype(BF16)
            for k in range(STEPS):
                now = jnp.where(step == k + 1, 1.0, 0.0)
                at[k * 192 : k * 192 + 192, cols] = times(hot, now)
            hot = jnp.where(lat_ids == lat[r : r + 1], 1.0, 0.0).astype(BF16)
            for p, piece in enumerate((w0, w1, v0, v1, v2)):
                bt[p * 256 : p * 256 + 256, cols] = times(hot, piece)
        acc[...] += lax.dot_general(
            at[...], bt[...], (((1,), (1,)), ((), ())), preferred_element_type=F32
        )
        return carry

    lax.fori_loop(0, (total + 7) // 8, group, 0)
    low = sublanes((8, 128)) < 4
    for k in range(STEPS):
        for l in range(LV):
            for u in range(2):
                rows = slice((k * LV + l) * COL, (k * LV + l + 1) * COL)
                take = lambda p: acc[rows, p * 256 + u * 128 : p * 256 + u * 128 + 128]
                w = take(0) + take(1)
                v = take(2) + take(3) + take(4)
                wsum[k, l, u] = w
                vsum[k, l, u] = v
                mix = jnp.where(low, w[16:24], pltpu.roll(v[16:24], 4, 0))
                lo = jnp.concatenate([w[:16], v[:16], mix], axis=0)
                mix = jnp.where(low, pltpu.roll(v[40:48], 4, 0), w[40:48])
                hi = jnp.concatenate([w[48:], v[48:], mix], axis=0)
                put_edges(sa, sb, (k, l, u), lo, hi, h)


def fetch(sources, buffers, sems):
    levels = []
    for l in range(LV):
        copies = []
        for i, (src, dst) in enumerate(zip(sources, buffers)):
            at = (slice(None), l) if len(src.shape) == 5 else l
            copies.append(pltpu.make_async_copy(src.at[at], dst.at[at], sems.at[l, i]))
        levels.append(copies)
        for copy in copies:
            copy.start()
    return levels


def hessian(p, wide, gains, drifts, n, s):
    e, seen = p, []
    for k in range(STEPS):
        e = tangent(e, gains(k), drifts(k), n, s)
        w = wide(k)
        seen.append([w[u] * e[u] for u in range(2)])
    x = None
    for k in reversed(range(STEPS)):
        x = seen[k] if x is None else [x[u] + seen[k][u] for u in range(2)]
        x = adjoint(x, gains(k), drifts(k), n, s)
    return [p[u] + x[u] for u in range(2)]


def core_kernel(
    ra, rb, w_in, v_in, states_in, gains_in, drifts_in, cn_in, cs_in, out, table_ref, *scratch
):
    *buffers, sems = scratch
    h = half()
    levels = fetch((w_in, v_in, states_in, gains_in, drifts_in, cn_in, cs_in), buffers, sems)
    wsum, vsum, states, gains, drifts, cn, cs = buffers
    sums = [jnp.zeros((8, 128), F32) for _ in range(5)]

    def fold(a, b):
        prod = a * b
        return jnp.sum(prod.reshape(8, 8, 128), axis=0)

    for l in range(LV):
        for copy in levels[l]:
            copy.wait()

        def window(ref, first):
            return lambda k: [ref[k, l, u, first : EXT - first] for u in range(2)]

        def still(ref, first):
            return [ref[l, u, first : EXT - first] for u in range(2)]

        def weights(first):
            def at(k):
                got = []
                for u in range(2):
                    left, right = get_edges(ra, rb, (k, l, u), h)
                    skip = first - 8
                    got.append(
                        jnp.concatenate(
                            [left[skip:16], wsum[k, l, u], right[: 16 - skip]], axis=0
                        )
                    )
                return got

            return at

        n, s = still(cn, 0), still(cs, 0)
        x = None
        for k in reversed(range(STEPS)):
            m = []
            for u in range(2):
                left, right = get_edges(ra, rb, (k, l, u), h)
                lm, rm = left[32:], right[32:]
                w = jnp.concatenate([lm, left[:16], wsum[k, l, u], right[:16], rm], axis=0)
                lm, rm = pltpu.roll(lm, 4, 0), pltpu.roll(rm, 4, 0)
                v = jnp.concatenate([lm, left[16:32], vsum[k, l, u], right[16:32], rm], axis=0)
                m.append(v - w * states[k, l, u])
            x = m if x is None else [x[u] + m[u] for u in range(2)]
            x = adjoint(x, window(gains, 0)(k), window(drifts, 0)(k), n, s)
        vectors = [x]
        for first in (8, 16):
            p = [x[u][8 : x[u].shape[0] - 8] for u in range(2)]
            x = hessian(
                p,
                weights(first),
                window(gains, first),
                window(drifts, first),
                still(cn, first),
                still(cs, first),
            )
            vectors.append(x)
        v = [
            [y[u][edge : edge + COL] for u in range(2)] for y, edge in zip(vectors, (24, 16, 8))
        ]
        for i, (a, b) in enumerate(((0, 0), (0, 1), (1, 1), (0, 2), (1, 2))):
            for u in range(2):
                sums[i] = sums[i] + fold(v[a][u], v[b][u])
        for i in range(3):
            for u in range(2):
                out[i * 3 + l, u] = v[i][u]
    lane = lanes((1, 128))
    table = jnp.zeros((1, 128), F32)
    for i in range(5):
        whole = jnp.sum(jnp.sum(sums[i], axis=0, keepdims=True), axis=1, keepdims=True)
        table = jnp.where(lane == i, whole, table)
    table_ref[...] = jnp.broadcast_to(table, (ALL, 128))


def turn_kernel(x, *refs):
    *outs, buf = refs
    me = lax.axis_index("lat")
    for f in range(9):
        buf[f] = jnp.concatenate([x[f, 0], x[f, 1]], axis=0).T
    for m, out in enumerate(outs):
        at = pl.ds(pl.multiple_of((me ^ m) * 16, 16), 16)
        for f in range(9):
            out[f] = buf[f, at, :]


def final_kernel(parts, *refs):
    *xs, increment, residual = refs
    total = jnp.sum(parts[...], axis=0, keepdims=True)
    lane = lanes((1, 128))
    pick = lambda i: jnp.sum(jnp.where(lane == i, total, 0.0), axis=1, keepdims=True)
    a00, a01, a11, a02, a12 = [jnp.broadcast_to(pick(i), (1, 128)) for i in range(5)]
    alpha = a00 / a01
    new = a00 - 2.0 * alpha * a01 + alpha * alpha * a11
    keep1 = 1.0 + new / a00
    curve = keep1 * (keep1 * a01 - alpha * (a02 + a11)) + alpha * alpha * a12
    second = new / curve
    a = alpha + second * keep1
    b = alpha * second
    low = lanes((16, 128)) < 64
    me = lax.axis_index("lat")
    first = jnp.full((16, 128), lax.rem(me, 2), I32) == 0
    for m in range(0, LAT, 2):
        q = (me ^ m) >> 1
        for l in range(LV):
            got = []
            for x in xs[m : m + 2]:
                v0, v1, v2 = x[l], x[3 + l], x[6 + l]
                got.append((a * v0 - b * v1, v0 - a * v1 + b * v2))
            for i, ref in enumerate((increment, residual)):
                x0 = jnp.where(first, got[0][i], got[1][i])
                x1 = jnp.where(first, got[1][i], got[0][i])
                level = 3 * q + l
                ref[level, pl.ds(0, 16, stride=2), :] = jnp.where(low, x0, pltpu.roll(x1, 64, 1))
                ref[level, pl.ds(1, 16, stride=2), :] = jnp.where(low, pltpu.roll(x0, 64, 1), x1)


VM = pl.BlockSpec(memory_space=pltpu.VMEM)
SM = pl.BlockSpec(memory_space=pltpu.SMEM)
AN = pl.BlockSpec(memory_space=pl.ANY)


def call(kernel, outs, *args, scratch=(), space="v", ins=None):
    shapes = tuple(
        pltpu.VMEM(s, F32) if where == "v" else jax.ShapeDtypeStruct(s, F32)
        for s, where in zip(outs, space * len(outs) if len(space) == 1 else space)
    )
    ins = ins or "v" * len(args)
    args = [
        pltpu.with_memory_space_constraint(a, pltpu.VMEM) if i == "v" else a
        for a, i in zip(args, ins)
    ]
    return make(kernel, shapes, ins, scratch)(*args)


def make(kernel, shapes, ins, scratch):
    return pl.pallas_call(
        kernel,
        out_shape=shapes if len(shapes) > 1 else shapes[0],
        in_specs=[{"s": SM, "a": AN}.get(i, VM) for i in ins],
        out_specs=(VM,) * len(shapes) if len(shapes) > 1 else VM,
        scratch_shapes=list(scratch),
    )


def swap(sa, sb):
    near, far = [], []
    for i in range(LAT):
        for j in range(LON):
            me = i * LON + j
            near.append((me, (i ^ 1) * LON + j))
            other = (j + 1) % LON if i % 2 else (j - 1) % LON
            far.append((me, (i ^ 1) * LON + other))
    rb = lax.ppermute(sb, ("lat", "lon"), far)
    ra = lax.ppermute(sa, ("lat", "lon"), near)
    return ra, rb


def exchange(blocks):
    got = [blocks[0]]
    for m in range(1, LAT):
        pairs = [(i * LON + j, (i ^ m) * LON + j) for i in range(LAT) for j in range(LON)]
        got.append(lax.ppermute(blocks[m], ("lat", "lon"), pairs))
    return got


def on_device(
    background, wind_lon, wind_lat, obs_value, obs_weight, obs_tile, obs_cell, obs_step, obs_count
):
    both = ("lat", "lon")
    plane = (LV, 2, EXT, 128)
    middle = (LV, 2, COL, 128)

    fold = lambda a: a.reshape(16, 128)
    packed = call(
        pack_kernel,
        [(ALL, 8, 128)],
        obs_count,
        fold(obs_tile),
        fold(obs_cell),
        fold(obs_step),
        fold(obs_value),
        fold(obs_weight),
        ins="shhhhh",
        scratch=[
            pltpu.VMEM((9, 16, 128), F32),
            pltpu.VMEM((2048, 128), BF16),
            pltpu.VMEM((2048, 256), F32),
            pltpu.VMEM((1024, 256), F32),
            pltpu.VMEM((1024, 2048), BF16),
            pltpu.VMEM((256, 2048), BF16),
        ],
    )
    arrived = lax.all_to_all(packed, both, 0, 0, tiled=True)
    blocks = call(prep_kernel, [(9, 16, 128)] * LAT, background, wind_lon, wind_lat, ins="hhh")
    blocks = exchange(blocks)
    fields, sa, sb = call(
        recv_kernel,
        [(9, 2, COL, 128)] + [(9, 2, EDGE, 128)] * 2,
        *blocks,
        space="hvv",
        scratch=[pltpu.VMEM((9, 128, 128), F32)],
    )
    ra, rb = swap(sa, sb)
    wsum, vsum, sa, sb = call(
        scatter_kernel,
        [(STEPS,) + middle] * 2 + [(STEPS, LV, 2, SLAB, 128)] * 2,
        arrived,
        space="hhvv",
        scratch=[
            pltpu.VMEM((4, 256, 128), F32),
            pltpu.VMEM((ROWS, 1024), BF16),
            pltpu.VMEM((1280, 1024), BF16),
            pltpu.VMEM((ROWS, 1280), F32),
        ],
    )
    wa, wb = swap(sa, sb)
    coefs = call(
        forward_kernel, [(STEPS,) + plane] * 3 + [plane] * 2, fields, ra, rb, ins="hvv", space="h"
    )
    big = pltpu.VMEM((STEPS,) + plane, F32)
    mid = pltpu.VMEM((STEPS,) + middle, F32)
    small = pltpu.VMEM(plane, F32)
    vectors, table = call(
        core_kernel,
        [(9, 2, COL, 128), (ALL, 128)],
        wa,
        wb,
        wsum,
        vsum,
        *coefs,
        ins="vv" + "a" * 7,
        scratch=[mid, mid, big, big, big, small, small, pltpu.SemaphoreType.DMA((LV, 7))],
    )
    parts = lax.all_to_all(table, both, 0, 0, tiled=True)
    blocks = call(
        turn_kernel, [(9, 16, 128)] * LAT, vectors, scratch=[pltpu.VMEM((9, 128, 128), F32)]
    )
    blocks = exchange(blocks)
    return call(final_kernel, [(12, 32, 128)] * 2, parts, *blocks, space="h")


def solution(mesh):
    grid = P(None, "lat", "lon")
    flat = P(("lat", "lon"))

    return jax.shard_map(
        on_device,
        mesh=mesh,
        in_specs=(grid, grid, grid, flat, flat, P(("lat", "lon"), None), flat, flat, flat),
        out_specs=(grid, grid),
        check_vma=False,
    )
```

```python
import jax
import jax.numpy as jnp
from jax import lax
from jax.experimental import pallas as pl
from jax.experimental.pallas import tpu as pltpu
from jax.sharding import PartitionSpec as P


LAT = 8
LON = 16
ALL = 128
STEPS = 4
LV = 3
COL = 64
EDGE = 24
EXT = COL + 2 * EDGE
SLAB = 40
ROOM = 256
SEG = 64
GROUP = 4
F32 = jnp.float32
BF16 = jnp.bfloat16
I32 = jnp.int32


def lanes(shape):
    return lax.broadcasted_iota(I32, shape, len(shape) - 1)


def sublanes(shape):
    return lax.broadcasted_iota(I32, shape, len(shape) - 2)


def half():
    return lax.rem(lax.axis_index("lat"), 2)


def prep_kernel(bg, wl, wt, keep, give):
    low = lanes((16, 128)) < 64
    h = half()
    for f, ref in enumerate((bg, wl, wt)):
        for level in range(12):
            q, l = level // 3, level % 3
            even = ref[level, pl.ds(0, 16, stride=2), :]
            odd = ref[level, pl.ds(1, 16, stride=2), :]
            first = jnp.where(low, even, pltpu.roll(odd, 64, 1))
            second = jnp.where(low, pltpu.roll(even, 64, 1), odd)

            @pl.when(h == 0)
            def _():
                keep[q, f * 3 + l] = first
                give[q, f * 3 + l] = second

            @pl.when(h != 0)
            def _():
                keep[q, f * 3 + l] = second
                give[q, f * 3 + l] = first


def merge_in_kernel(keep, got, *outs):
    h = half()
    x = lax.axis_index("lat") >> 1
    for t, out in enumerate(outs):
        out[h] = keep[x ^ t]
        out[1 - h] = got[x ^ t]


def put_edges(sa, sb, index, lo, hi, h):
    @pl.when(h == 0)
    def _():
        sa[index] = hi
        sb[index] = lo

    @pl.when(h != 0)
    def _():
        sa[index] = lo
        sb[index] = hi


def get_edges(ra, rb, index, h):
    a, b = ra[index], rb[index]
    first = jnp.full(a.shape, h, I32) == 0
    return jnp.where(first, b, a), jnp.where(first, a, b)


def recv_kernel(*refs):
    *xs, center, sa, sb, buf = refs
    h = half()
    mine = lax.axis_index("lat") >> 1
    for t, x in enumerate(xs):
        for c in range(2):
            at = pl.ds(pl.multiple_of((mine ^ t) * 32 + c * 16, 16), 16)
            for f in range(9):
                buf[f, at, :] = x[c, f]
    for f in range(9):
        t = buf[f].T
        for u in range(2):
            center[f, u] = t[u * 64 : u * 64 + 64]
            lo = t[u * 64 : u * 64 + EDGE]
            hi = t[u * 64 + COL - EDGE : u * 64 + COL]
            put_edges(sa, sb, (f, u), lo, hi, h)


def up(x):
    return pltpu.roll(x, x.shape[0] - 1, 0)


def down(x):
    return pltpu.roll(x, 1, 0)


def north(e, o):
    return pltpu.roll(o, 1, 1), e


def south(e, o):
    return o, pltpu.roll(e, 127, 1)


def forward_kernel(center, ra, rb, states, gains, drifts, cn, cs):
    h = half()
    lane = lanes((EXT, 128))

    def ext(f, u):
        left, right = get_edges(ra, rb, (f, u), h)
        return jnp.concatenate([left, center[f, u], right], axis=0)

    for l in range(LV):
        s = [ext(l, u) for u in range(2)]
        wl = [ext(3 + l, u) for u in range(2)]
        wt = [ext(6 + l, u) for u in range(2)]
        n = [0.08 + 0.5 * wt[u] for u in range(2)]
        d = [0.08 - 0.5 * wt[u] for u in range(2)]
        n[0] = jnp.where(lane == 0, 0.0, n[0])
        d[1] = jnp.where(lane == 127, 0.0, d[1])
        for u in range(2):
            cn[l, u] = n[u]
            cs[l, u] = d[u]
        for k in range(STEPS):
            no, so = north(*s), south(*s)
            new = []
            for u in range(2):
                hi, lo = up(s[u]), down(s[u])
                drift = 0.5 * wl[u] + 0.1 * s[u]
                gains[k, l, u] = 0.68 - 0.1 * (hi - lo)
                drifts[k, l, u] = drift
                new.append(
                    0.68 * s[u] + 0.08 * (hi + lo) - drift * (hi - lo) + n[u] * no[u] + d[u] * so[u]
                )
            s = new
            for u in range(2):
                states[k, l, u] = s[u]


def tangent(e, g, d, n, s):
    no, so = north(*e), south(*e)
    out = []
    for u in range(2):
        hi, lo = up(e[u]), down(e[u])
        out.append(g[u] * e[u] + 0.08 * (hi + lo) - d[u] * (hi - lo) + n[u] * no[u] + s[u] * so[u])
    return out


def adjoint(x, g, d, n, s):
    no = north(s[0] * x[0], s[1] * x[1])
    so = south(n[0] * x[0], n[1] * x[1])
    out = []
    for u in range(2):
        flow = d[u] * x[u]
        wide = 0.08 * x[u]
        out.append(g[u] * x[u] + up(wide + flow) + down(wide - flow) + no[u] + so[u])
    return out


def pack_kernel(count, tile, cell, step, value, weight, out, rows, member, counted, acc, left, right):
    shape = (16, 128)
    live = sublanes(shape) * 128 + lanes(shape) < count[0]
    c, t = cell[...], tile[...]
    level = c >> 12
    q = (level >= 3).astype(I32) + (level >= 6).astype(I32) + (level >= 9).astype(I32)
    row = (c & 4095) >> 7
    col = c & 127
    lat = (t >> 4) * 32 + row
    dest = (2 * q + (col >> 6)) * LON + (t & 15)
    w = jnp.where(live, weight[...], 0.0)
    w0 = w.astype(BF16).astype(F32)
    w1 = (w - w0).astype(BF16).astype(F32)
    wv = (w0 + w1) * value[...]
    v0 = wv.astype(BF16).astype(F32)
    v1 = (wv - v0).astype(BF16).astype(F32)
    rows[0] = jnp.where(live, dest, -1).astype(F32)
    rows[1] = (((level - 3 * q) * 64 + (col & 63)) * 256).astype(F32)
    rows[2] = ((lat & 1) * 128 + (lat >> 1)).astype(F32)
    rows[3] = step[...].astype(F32)
    rows[4] = w0
    rows[5] = w1
    rows[6] = v0
    rows[7] = v1
    rows[8] = wv - v0 - v1
    square = (128, 256)
    before = ((sublanes(square) < lanes(square)) | (lanes(square) >= 128)).astype(F32).astype(BF16)
    ids = sublanes((128, 128)).astype(F32)
    places = sublanes((ROOM, 128)).astype(F32)
    for b in range(16):
        at = slice(b * 128, b * 128 + 128)
        mine = ids == rows[0, b : b + 1, :]
        member[at, :] = jnp.where(mine, 1.0, 0.0).astype(BF16)
        for p in range(8):
            piece = rows[1 + p, b : b + 1, :]
            left[p * 128 : p * 128 + 128, at] = jnp.where(mine, piece, 0.0).astype(BF16)
    counted[...] = jnp.dot(member[...], before, preferred_element_type=F32)
    base = jnp.zeros((128, 128), F32)
    for b in range(16):
        at = slice(b * 128, b * 128 + 128)
        mine = ids == rows[0, b : b + 1, :]
        rank = jnp.where(mine, counted[at, :128] + base, 0.0)
        rank = jnp.sum(rank, axis=0, keepdims=True)
        base = base + counted[at, 128:]
        right[:, at] = jnp.where(places == rank, 1.0, 0.0).astype(BF16)
    acc[...] = lax.dot_general(
        left[...], right[...], (((1,), (1,)), ((), ())), preferred_element_type=F32
    )
    for ch, pieces in enumerate(((0, 1), (2,), (3, 4), (5, 6, 7))):
        for hf in range(2):
            at = slice(hf * 128, hf * 128 + 128)
            out[:, 2 * ch + hf, :] = sum(acc[p * 128 : p * 128 + 128, at] for p in pieces)


def scatter_kernel(x, wsum, vsum, sa, sb, xt, sorted_, at, bt, acc):
    h = half()
    most = jnp.max(x[:, 2:4, :], axis=0)
    total = jnp.sum(jnp.where(most > 0.5, 1.0, 0.0)).astype(I32)
    acc[...] = jnp.zeros_like(acc)
    for ch in range(4):
        xt[ch, :128] = x[:, 2 * ch, :].T

    @pl.when(total > 128)
    def _():
        for ch in range(4):
            xt[ch, 128:] = x[:, 2 * ch + 1, :].T

    block = (SEG, 128)
    place = sublanes(block)
    square = (SEG, SEG)
    before = (lanes(square) < sublanes(square)).astype(F32).astype(BF16)
    row_ids = sublanes((LV * COL, 128))
    lat_ids = sublanes((256, 128))

    def line(ref):
        return jnp.broadcast_to(ref, (16, 128)).astype(BF16)

    def times(hot, scale):
        return (hot.reshape(-1, 16, 128) * scale[None]).reshape(-1, 128)

    def segment(i, carry):
        first = pl.multiple_of(i * SEG, SEG)
        part = lambda ch: xt[ch, pl.ds(first, SEG), :]
        step = part(1)
        for k in range(STEPS):
            valid = jnp.where(step == k + 1.0, 1.0, 0.0)
            count = jnp.sum(valid, axis=0, keepdims=True)
            ahead = jnp.dot(before, valid.astype(BF16), preferred_element_type=F32).astype(I32)
            shift = jnp.where(step == k + 1.0, place - ahead, 0)
            moved = [part(0), part(2), part(3)]
            for bit in (1, 2, 4, 8, 16, 32):
                go = shift & bit
                come = pltpu.roll(go, SEG - bit, 0) != 0
                moved = [jnp.where(come, pltpu.roll(y, SEG - bit, 0), y) for y in moved]
                shift = jnp.where(
                    come, pltpu.roll(shift, SEG - bit, 0), jnp.where(go != 0, 0, shift)
                )
            there = place < count.astype(I32)
            cell = moved[0].astype(I32)
            w = jnp.where(there, moved[1], 0.0)
            v = jnp.where(there, moved[2], 0.0)
            w0 = w.astype(BF16).astype(F32)
            v0 = v.astype(BF16).astype(F32)
            v1 = (v - v0).astype(BF16).astype(F32)
            pieces = ((cell >> 8).astype(F32), (cell & 255).astype(F32), w0, w - w0, v0, v1, v - v0 - v1)
            for n, piece in enumerate(pieces):
                sorted_[n] = piece
            longest = jnp.max(count).astype(I32)

            def group(g, carry):
                for r in range(GROUP):
                    cols = slice(r * 128, r * 128 + 128)
                    get = lambda n: sorted_[n, pl.ds(g * GROUP + r, 1), :]
                    hot = jnp.where(row_ids == get(0).astype(I32), 1.0, 0.0).astype(BF16)
                    for p in range(5):
                        at[p * 192 : p * 192 + 192, cols] = times(hot, line(get(2 + p)))
                    bt[:, cols] = jnp.where(lat_ids == get(1).astype(I32), 1.0, 0.0).astype(BF16)
                acc[k * 960 : k * 960 + 960, :] += lax.dot_general(
                    at[...], bt[...], (((1,), (1,)), ((), ())), preferred_element_type=F32
                )
                return carry

            lax.fori_loop(0, (longest + GROUP - 1) // GROUP, group, 0)
        return carry

    lax.fori_loop(0, (total + SEG - 1) // SEG, segment, 0)
    low = sublanes((8, 128)) < 4
    for k in range(STEPS):
        for l in range(LV):
            for u in range(2):
                top = k * 960 + l * COL

                def take(p):
                    return acc[top + p * 192 : top + p * 192 + COL, u * 128 : u * 128 + 128]

                w = take(0) + take(1)
                v = take(2) + take(3) + take(4)
                wsum[k, l, u] = w
                vsum[k, l, u] = v
                mix = jnp.where(low, w[16:24], pltpu.roll(v[16:24], 4, 0))
                lo = jnp.concatenate([w[:16], v[:16], mix], axis=0)
                mix = jnp.where(low, pltpu.roll(v[40:48], 4, 0), w[40:48])
                hi = jnp.concatenate([w[48:], v[48:], mix], axis=0)
                put_edges(sa, sb, (k, l, u), lo, hi, h)


def fetch(sources, buffers, sems):
    levels = []
    for l in range(LV):
        copies = []
        for i, (src, dst) in enumerate(zip(sources, buffers)):
            at = (slice(None), l) if len(src.shape) == 5 else l
            copies.append(pltpu.make_async_copy(src.at[at], dst.at[at], sems.at[l, i]))
        levels.append(copies)
        for copy in copies:
            copy.start()
    return levels


def hessian(p, wide, gains, drifts, n, s):
    e, seen = p, []
    for k in range(STEPS):
        e = tangent(e, gains(k), drifts(k), n, s)
        w = wide(k)
        seen.append([w[u] * e[u] for u in range(2)])
    x = None
    for k in reversed(range(STEPS)):
        x = seen[k] if x is None else [x[u] + seen[k][u] for u in range(2)]
        x = adjoint(x, gains(k), drifts(k), n, s)
    return [p[u] + x[u] for u in range(2)]


def core_kernel(
    ra, rb, w_in, v_in, states_in, gains_in, drifts_in, cn_in, cs_in, out, table_ref, *scratch
):
    *buffers, sems = scratch
    h = half()
    levels = fetch((w_in, v_in, states_in, gains_in, drifts_in, cn_in, cs_in), buffers, sems)
    wsum, vsum, states, gains, drifts, cn, cs = buffers
    sums = [jnp.zeros((8, 128), F32) for _ in range(5)]

    def fold(a, b):
        prod = a * b
        return jnp.sum(prod.reshape(8, 8, 128), axis=0)

    for l in range(LV):
        for copy in levels[l]:
            copy.wait()

        def window(ref, first):
            return lambda k: [ref[k, l, u, first : EXT - first] for u in range(2)]

        def still(ref, first):
            return [ref[l, u, first : EXT - first] for u in range(2)]

        def weights(first):
            def at(k):
                got = []
                for u in range(2):
                    left, right = get_edges(ra, rb, (k, l, u), h)
                    skip = first - 8
                    got.append(
                        jnp.concatenate(
                            [left[skip:16], wsum[k, l, u], right[: 16 - skip]], axis=0
                        )
                    )
                return got

            return at

        n, s = still(cn, 0), still(cs, 0)
        x = None
        for k in reversed(range(STEPS)):
            m = []
            for u in range(2):
                left, right = get_edges(ra, rb, (k, l, u), h)
                lm, rm = left[32:], right[32:]
                w = jnp.concatenate([lm, left[:16], wsum[k, l, u], right[:16], rm], axis=0)
                lm, rm = pltpu.roll(lm, 4, 0), pltpu.roll(rm, 4, 0)
                v = jnp.concatenate([lm, left[16:32], vsum[k, l, u], right[16:32], rm], axis=0)
                m.append(v - w * states[k, l, u])
            x = m if x is None else [x[u] + m[u] for u in range(2)]
            x = adjoint(x, window(gains, 0)(k), window(drifts, 0)(k), n, s)
        vectors = [x]
        for first in (8, 16):
            p = [x[u][8 : x[u].shape[0] - 8] for u in range(2)]
            x = hessian(
                p,
                weights(first),
                window(gains, first),
                window(drifts, first),
                still(cn, first),
                still(cs, first),
            )
            vectors.append(x)
        v = [
            [y[u][edge : edge + COL] for u in range(2)] for y, edge in zip(vectors, (24, 16, 8))
        ]
        for i, (a, b) in enumerate(((0, 0), (0, 1), (1, 1), (0, 2), (1, 2))):
            for u in range(2):
                sums[i] = sums[i] + fold(v[a][u], v[b][u])
        for i in range(3):
            for u in range(2):
                out[i * 3 + l, u] = v[i][u]
    lane = lanes((1, 128))
    table = jnp.zeros((1, 128), F32)
    for i in range(5):
        whole = jnp.sum(jnp.sum(sums[i], axis=0, keepdims=True), axis=1, keepdims=True)
        table = jnp.where(lane == i, whole, table)
    table_ref[...] = jnp.broadcast_to(table, (ALL, 128))


def turn_kernel(x, keep, give):
    h = half()
    for f in range(9):
        t = jnp.concatenate([x[f, 0], x[f, 1]], axis=0).T
        for n in range(4):
            first, second = t[n * 32 : n * 32 + 16], t[n * 32 + 16 : n * 32 + 32]

            @pl.when(h == 0)
            def _():
                keep[n, f] = first
                give[n, f] = second

            @pl.when(h != 0)
            def _():
                keep[n, f] = second
                give[n, f] = first


def merge_out_kernel(keep, got, *outs):
    h = half()
    x = lax.axis_index("lat") >> 1
    low = lanes((16, 128)) < 64
    first = jnp.full((16, 128), h, I32) == 0
    for t, out in enumerate(outs):
        for f in range(9):
            a, b = keep[x ^ t, f], got[x ^ t, f]
            x0, x1 = jnp.where(first, a, b), jnp.where(first, b, a)
            out[f, pl.ds(0, 16, stride=2), :] = jnp.where(low, x0, pltpu.roll(x1, 64, 1))
            out[f, pl.ds(1, 16, stride=2), :] = jnp.where(low, pltpu.roll(x0, 64, 1), x1)


def final_kernel(parts, *refs):
    *xs, increment, residual = refs
    total = jnp.sum(parts[...], axis=0, keepdims=True)
    lane = lanes((1, 128))
    pick = lambda i: jnp.sum(jnp.where(lane == i, total, 0.0), axis=1, keepdims=True)
    a00, a01, a11, a02, a12 = [jnp.broadcast_to(pick(i), (1, 128)) for i in range(5)]
    alpha = a00 / a01
    new = a00 - 2.0 * alpha * a01 + alpha * alpha * a11
    keep1 = 1.0 + new / a00
    curve = keep1 * (keep1 * a01 - alpha * (a02 + a11)) + alpha * alpha * a12
    second = new / curve
    a = alpha + second * keep1
    b = alpha * second
    mine = lax.axis_index("lat") >> 1
    for t, x in enumerate(xs):
        for l in range(LV):
            v0, v1, v2 = x[l], x[3 + l], x[6 + l]
            level = 3 * (mine ^ t) + l
            increment[level] = a * v0 - b * v1
            residual[level] = v0 - a * v1 + b * v2


VM = pl.BlockSpec(memory_space=pltpu.VMEM)
SM = pl.BlockSpec(memory_space=pltpu.SMEM)
AN = pl.BlockSpec(memory_space=pl.ANY)


def call(kernel, outs, *args, scratch=(), space="v", ins=None):
    shapes = tuple(
        pltpu.VMEM(s, F32) if where == "v" else jax.ShapeDtypeStruct(s, F32)
        for s, where in zip(outs, space * len(outs) if len(space) == 1 else space)
    )
    ins = ins or "v" * len(args)
    args = [
        pltpu.with_memory_space_constraint(a, pltpu.VMEM) if i == "v" else a
        for a, i in zip(args, ins)
    ]
    return make(kernel, shapes, ins, scratch)(*args)


def make(kernel, shapes, ins, scratch):
    return pl.pallas_call(
        kernel,
        out_shape=shapes if len(shapes) > 1 else shapes[0],
        in_specs=[{"s": SM, "a": AN}.get(i, VM) for i in ins],
        out_specs=(VM,) * len(shapes) if len(shapes) > 1 else VM,
        scratch_shapes=list(scratch),
    )


def swap(sa, sb):
    near, far = [], []
    for i in range(LAT):
        for j in range(LON):
            me = i * LON + j
            near.append((me, (i ^ 1) * LON + j))
            other = (j + 1) % LON if i % 2 else (j - 1) % LON
            far.append((me, (i ^ 1) * LON + other))
    rb = lax.ppermute(sb, ("lat", "lon"), far)
    ra = lax.ppermute(sa, ("lat", "lon"), near)
    return ra, rb


def flip(x, bits):
    pairs = [(i * LON + j, (i ^ bits) * LON + j) for i in range(LAT) for j in range(LON)]
    return lax.ppermute(x, ("lat", "lon"), pairs)


def ring(blocks):
    return [blocks[0]] + [flip(blocks[t], 2 * t) for t in range(1, 4)]


def on_device(
    background, wind_lon, wind_lat, obs_value, obs_weight, obs_tile, obs_cell, obs_step, obs_count
):
    both = ("lat", "lon")
    plane = (LV, 2, EXT, 128)
    middle = (LV, 2, COL, 128)

    group = (4, 9, 16, 128)
    keep, give = call(prep_kernel, [group] * 2, background, wind_lon, wind_lat, ins="hhh")
    got = flip(give, 1)
    fold = lambda a: a.reshape(16, 128)
    packed = call(
        pack_kernel,
        [(ALL, 8, 128)],
        obs_count,
        fold(obs_tile),
        fold(obs_cell),
        fold(obs_step),
        fold(obs_value),
        fold(obs_weight),
        ins="shhhhh",
        scratch=[
            pltpu.VMEM((9, 16, 128), F32),
            pltpu.VMEM((2048, 128), BF16),
            pltpu.VMEM((2048, 256), F32),
            pltpu.VMEM((1024, 256), F32),
            pltpu.VMEM((1024, 2048), BF16),
            pltpu.VMEM((256, 2048), BF16),
        ],
    )
    arrived = lax.all_to_all(packed, both, 0, 0, tiled=True)
    blocks = ring(call(merge_in_kernel, [(2, 9, 16, 128)] * 4, keep, got))
    fields, sa, sb = call(
        recv_kernel,
        [(9, 2, COL, 128)] + [(9, 2, EDGE, 128)] * 2,
        *blocks,
        space="hvv",
        scratch=[pltpu.VMEM((9, 128, 128), F32)],
    )
    ra, rb = swap(sa, sb)
    wsum, vsum, sa, sb = call(
        scatter_kernel,
        [(STEPS,) + middle] * 2 + [(STEPS, LV, 2, SLAB, 128)] * 2,
        arrived,
        space="hhvv",
        scratch=[
            pltpu.VMEM((4, 256, 128), F32),
            pltpu.VMEM((7, SEG, 128), F32),
            pltpu.VMEM((5 * LV * COL, GROUP * 128), BF16),
            pltpu.VMEM((256, GROUP * 128), BF16),
            pltpu.VMEM((STEPS * 5 * LV * COL, 256), F32),
        ],
    )
    wa, wb = swap(sa, sb)
    coefs = call(
        forward_kernel, [(STEPS,) + plane] * 3 + [plane] * 2, fields, ra, rb, ins="hvv", space="h"
    )
    big = pltpu.VMEM((STEPS,) + plane, F32)
    mid = pltpu.VMEM((STEPS,) + middle, F32)
    small = pltpu.VMEM(plane, F32)
    vectors, table = call(
        core_kernel,
        [(9, 2, COL, 128), (ALL, 128)],
        wa,
        wb,
        wsum,
        vsum,
        *coefs,
        ins="vv" + "a" * 7,
        scratch=[mid, mid, big, big, big, small, small, pltpu.SemaphoreType.DMA((LV, 7))],
    )
    keep, give = call(turn_kernel, [group] * 2, vectors)
    got = flip(give, 1)
    parts = lax.all_to_all(table, both, 0, 0, tiled=True)
    blocks = ring(call(merge_out_kernel, [(9, 32, 128)] * 4, keep, got))
    return call(final_kernel, [(12, 32, 128)] * 2, parts, *blocks, space="h")


def solution(mesh):
    grid = P(None, "lat", "lon")
    flat = P(("lat", "lon"))

    return jax.shard_map(
        on_device,
        mesh=mesh,
        in_specs=(grid, grid, grid, flat, flat, P(("lat", "lon"), None), flat, flat, flat),
        out_specs=(grid, grid),
        check_vma=False,
    )
```

```python
import jax
import jax.numpy as jnp
from jax import lax
from jax.experimental import pallas as pl
from jax.experimental.pallas import tpu as pltpu
from jax.sharding import PartitionSpec as P


LAT = 8
LON = 16
ALL = 128
STEPS = 4
LV = 3
COL = 64
EDGE = 24
EXT = COL + 2 * EDGE
SLAB = 40
ROOM = 256
SEG = 64
GROUP = 4
F32 = jnp.float32
BF16 = jnp.bfloat16
I32 = jnp.int32


def lanes(shape):
    return lax.broadcasted_iota(I32, shape, len(shape) - 1)


def sublanes(shape):
    return lax.broadcasted_iota(I32, shape, len(shape) - 2)


def half():
    return lax.rem(lax.axis_index("lat"), 2)


def sort_halves(h, x, y):
    first = jnp.full(x.shape, h, I32) == 0
    return jnp.where(first, x, y), jnp.where(first, y, x)


def prep_kernel(bg, wl, wt, keep, give):
    low = lanes((16, 128)) < 64
    h = half()
    for f, ref in enumerate((bg, wl, wt)):
        for level in range(12):
            q, l = level // 3, level % 3
            even = ref[level, pl.ds(0, 16, stride=2), :]
            odd = ref[level, pl.ds(1, 16, stride=2), :]
            x = jnp.where(low, even, pltpu.roll(odd, 64, 1))
            y = jnp.where(low, pltpu.roll(even, 64, 1), odd)
            keep[q, f * 3 + l], give[q, f * 3 + l] = sort_halves(h, x, y)


def merge_in_kernel(keep, got, *outs):
    h = half()
    x = lax.axis_index("lat") >> 1
    for t, out in enumerate(outs):
        out[h] = keep[x ^ t]
        out[1 - h] = got[x ^ t]


def put_edges(sa, sb, index, lo, hi, h):
    sa[index], sb[index] = sort_halves(h, hi, lo)


def get_edges(ra, rb, index, h):
    return sort_halves(h, rb[index], ra[index])


def recv_kernel(*refs):
    *xs, center, sa, sb, buf = refs
    h = half()
    mine = lax.axis_index("lat") >> 1
    for t, x in enumerate(xs):
        for c in range(2):
            at = pl.ds(pl.multiple_of((mine ^ t) * 32 + c * 16, 16), 16)
            for f in range(9):
                buf[f, at, :] = x[c, f]
    for f in range(9):
        t = buf[f].T
        for u in range(2):
            center[f, u] = t[u * 64 : u * 64 + 64]
            lo = t[u * 64 : u * 64 + EDGE]
            hi = t[u * 64 + COL - EDGE : u * 64 + COL]
            put_edges(sa, sb, (f, u), lo, hi, h)


def up(x):
    return pltpu.roll(x, x.shape[0] - 1, 0)


def down(x):
    return pltpu.roll(x, 1, 0)


def north(e, o):
    return pltpu.roll(o, 1, 1), e


def south(e, o):
    return o, pltpu.roll(e, 127, 1)


def forward_kernel(center, ra, rb, states, gains, drifts, cn, cs):
    h = half()
    lane = lanes((EXT, 128))

    def ext(f, u):
        left, right = get_edges(ra, rb, (f, u), h)
        return jnp.concatenate([left, center[f, u], right], axis=0)

    for l in range(LV):
        s = [ext(l, u) for u in range(2)]
        wl = [ext(3 + l, u) for u in range(2)]
        wt = [ext(6 + l, u) for u in range(2)]
        n = [0.08 + 0.5 * wt[u] for u in range(2)]
        d = [0.08 - 0.5 * wt[u] for u in range(2)]
        n[0] = jnp.where(lane == 0, 0.0, n[0])
        d[1] = jnp.where(lane == 127, 0.0, d[1])
        for u in range(2):
            cn[l, u] = n[u]
            cs[l, u] = d[u]
        for k in range(STEPS):
            no, so = north(*s), south(*s)
            new = []
            for u in range(2):
                hi, lo = up(s[u]), down(s[u])
                drift = 0.5 * wl[u] + 0.1 * s[u]
                gains[k, l, u] = 0.68 - 0.1 * (hi - lo)
                drifts[k, l, u] = drift
                new.append(
                    0.68 * s[u] + 0.08 * (hi + lo) - drift * (hi - lo) + n[u] * no[u] + d[u] * so[u]
                )
            s = new
            for u in range(2):
                states[k, l, u] = s[u]


def tangent(e, g, d, n, s):
    no, so = north(*e), south(*e)
    out = []
    for u in range(2):
        hi, lo = up(e[u]), down(e[u])
        out.append(g[u] * e[u] + 0.08 * (hi + lo) - d[u] * (hi - lo) + n[u] * no[u] + s[u] * so[u])
    return out


def adjoint(x, g, d, n, s):
    no = north(s[0] * x[0], s[1] * x[1])
    so = south(n[0] * x[0], n[1] * x[1])
    out = []
    for u in range(2):
        flow = d[u] * x[u]
        wide = 0.08 * x[u]
        out.append(g[u] * x[u] + up(wide + flow) + down(wide - flow) + no[u] + so[u])
    return out


def pack_kernel(count, tile, cell, step, value, weight, out, rows, member, counted, acc, left, right):
    shape = (16, 128)
    live = sublanes(shape) * 128 + lanes(shape) < count[0]
    c, t = cell[...], tile[...]
    level = c >> 12
    q = (level >= 3).astype(I32) + (level >= 6).astype(I32) + (level >= 9).astype(I32)
    row = (c & 4095) >> 7
    col = c & 127
    lat = (t >> 4) * 32 + row
    dest = (2 * q + (col >> 6)) * LON + (t & 15)
    w = jnp.where(live, weight[...], 0.0)
    w0 = w.astype(BF16).astype(F32)
    w1 = (w - w0).astype(BF16).astype(F32)
    wv = (w0 + w1) * value[...]
    v0 = wv.astype(BF16).astype(F32)
    v1 = (wv - v0).astype(BF16).astype(F32)
    rows[0] = jnp.where(live, dest, -1).astype(F32)
    rows[1] = (((level - 3 * q) * 64 + (col & 63)) * 256).astype(F32)
    rows[2] = ((lat & 1) * 128 + (lat >> 1)).astype(F32)
    rows[3] = step[...].astype(F32)
    rows[4] = w0
    rows[5] = w1
    rows[6] = v0
    rows[7] = v1
    rows[8] = wv - v0 - v1
    square = (128, 256)
    before = ((sublanes(square) < lanes(square)) | (lanes(square) >= 128)).astype(F32).astype(BF16)
    ids = sublanes((128, 128)).astype(F32)
    places = sublanes((ROOM, 128)).astype(F32)
    for b in range(16):
        at = slice(b * 128, b * 128 + 128)
        mine = ids == rows[0, b : b + 1, :]
        member[at, :] = jnp.where(mine, 1.0, 0.0).astype(BF16)
        for p in range(8):
            piece = rows[1 + p, b : b + 1, :]
            left[p * 128 : p * 128 + 128, at] = jnp.where(mine, piece, 0.0).astype(BF16)
    counted[...] = jnp.dot(member[...], before, preferred_element_type=F32)
    base = jnp.zeros((128, 128), F32)
    for b in range(16):
        at = slice(b * 128, b * 128 + 128)
        mine = ids == rows[0, b : b + 1, :]
        rank = jnp.where(mine, counted[at, :128] + base, 0.0)
        rank = jnp.sum(rank, axis=0, keepdims=True)
        base = base + counted[at, 128:]
        right[:, at] = jnp.where(places == rank, 1.0, 0.0).astype(BF16)
    acc[...] = lax.dot_general(
        left[...], right[...], (((1,), (1,)), ((), ())), preferred_element_type=F32
    )
    for ch, pieces in enumerate(((0, 1), (2,), (3, 4), (5, 6, 7))):
        for hf in range(2):
            at = slice(hf * 128, hf * 128 + 128)
            out[:, 2 * ch + hf, :] = sum(acc[p * 128 : p * 128 + 128, at] for p in pieces)


def scatter_kernel(x, wsum, vsum, sa, sb, xt, sorted_, at, bt, acc):
    h = half()
    most = jnp.max(x[:, 2:4, :], axis=0)
    total = jnp.sum(jnp.where(most > 0.5, 1.0, 0.0)).astype(I32)
    acc[...] = jnp.zeros_like(acc)
    for ch in range(4):
        xt[ch, :128] = x[:, 2 * ch, :].T

    @pl.when(total > 128)
    def _():
        for ch in range(4):
            xt[ch, 128:] = x[:, 2 * ch + 1, :].T

    block = (SEG, 128)
    place = sublanes(block)
    square = (SEG, SEG)
    before = (lanes(square) < sublanes(square)).astype(F32).astype(BF16)
    row_ids = sublanes((LV * COL, 128))
    lat_ids = sublanes((256, 128))

    def line(ref):
        return jnp.broadcast_to(ref, (16, 128)).astype(BF16)

    def times(hot, scale):
        return (hot.reshape(-1, 16, 128) * scale[None]).reshape(-1, 128)

    def segment(i, carry):
        first = pl.multiple_of(i * SEG, SEG)
        part = lambda ch: xt[ch, pl.ds(first, SEG), :]
        step = part(1)
        for k in range(STEPS):
            valid = jnp.where(step == k + 1.0, 1.0, 0.0)
            count = jnp.sum(valid, axis=0, keepdims=True)
            ahead = jnp.dot(before, valid.astype(BF16), preferred_element_type=F32).astype(I32)
            shift = jnp.where(step == k + 1.0, place - ahead, 0)
            moved = [part(0), part(2), part(3)]
            for bit in (1, 2, 4, 8, 16, 32):
                go = shift & bit
                come = pltpu.roll(go, SEG - bit, 0) != 0
                moved = [jnp.where(come, pltpu.roll(y, SEG - bit, 0), y) for y in moved]
                shift = jnp.where(
                    come, pltpu.roll(shift, SEG - bit, 0), jnp.where(go != 0, 0, shift)
                )
            there = place < count.astype(I32)
            cell = moved[0].astype(I32)
            w = jnp.where(there, moved[1], 0.0)
            v = jnp.where(there, moved[2], 0.0)
            w0 = w.astype(BF16).astype(F32)
            v0 = v.astype(BF16).astype(F32)
            v1 = (v - v0).astype(BF16).astype(F32)
            pieces = ((cell >> 8).astype(F32), (cell & 255).astype(F32), w0, w - w0, v0, v1, v - v0 - v1)
            for n, piece in enumerate(pieces):
                sorted_[n] = piece
            longest = jnp.max(count).astype(I32)

            def group(g, carry):
                for r in range(GROUP):
                    cols = slice(r * 128, r * 128 + 128)
                    get = lambda n: sorted_[n, pl.ds(g * GROUP + r, 1), :]
                    hot = jnp.where(row_ids == get(0).astype(I32), 1.0, 0.0).astype(BF16)
                    for p in range(5):
                        at[p * 192 : p * 192 + 192, cols] = times(hot, line(get(2 + p)))
                    bt[:, cols] = jnp.where(lat_ids == get(1).astype(I32), 1.0, 0.0).astype(BF16)
                acc[k * 960 : k * 960 + 960, :] += lax.dot_general(
                    at[...], bt[...], (((1,), (1,)), ((), ())), preferred_element_type=F32
                )
                return carry

            lax.fori_loop(0, (longest + GROUP - 1) // GROUP, group, 0)
        return carry

    lax.fori_loop(0, (total + SEG - 1) // SEG, segment, 0)
    low = sublanes((8, 128)) < 4
    for k in range(STEPS):
        for l in range(LV):
            for u in range(2):
                top = k * 960 + l * COL

                def take(p):
                    return acc[top + p * 192 : top + p * 192 + COL, u * 128 : u * 128 + 128]

                w = take(0) + take(1)
                v = take(2) + take(3) + take(4)
                wsum[k, l, u] = w
                vsum[k, l, u] = v
                mix = jnp.where(low, w[16:24], pltpu.roll(v[16:24], 4, 0))
                lo = jnp.concatenate([w[:16], v[:16], mix], axis=0)
                mix = jnp.where(low, pltpu.roll(v[40:48], 4, 0), w[40:48])
                hi = jnp.concatenate([w[48:], v[48:], mix], axis=0)
                put_edges(sa, sb, (k, l, u), lo, hi, h)


def fetch(sources, buffers, sems):
    levels = []
    for l in range(LV):
        copies = []
        for i, (src, dst) in enumerate(zip(sources, buffers)):
            at = (slice(None), l) if len(src.shape) == 5 else l
            copies.append(pltpu.make_async_copy(src.at[at], dst.at[at], sems.at[l, i]))
        levels.append(copies)
        for copy in copies:
            copy.start()
    return levels


def hessian(p, wide, gains, drifts, n, s):
    e, seen = p, []
    for k in range(STEPS):
        e = tangent(e, gains(k), drifts(k), n, s)
        w = wide(k)
        seen.append([w[u] * e[u] for u in range(2)])
    x = None
    for k in reversed(range(STEPS)):
        x = seen[k] if x is None else [x[u] + seen[k][u] for u in range(2)]
        x = adjoint(x, gains(k), drifts(k), n, s)
    return [p[u] + x[u] for u in range(2)]


def core_kernel(
    ra, rb, w_in, v_in, states_in, gains_in, drifts_in, cn_in, cs_in, out, table_ref, *scratch
):
    *buffers, sems = scratch
    h = half()
    levels = fetch((w_in, v_in, states_in, gains_in, drifts_in, cn_in, cs_in), buffers, sems)
    wsum, vsum, states, gains, drifts, cn, cs = buffers
    sums = [jnp.zeros((8, 128), F32) for _ in range(5)]

    def fold(a, b):
        prod = a * b
        return jnp.sum(prod.reshape(8, 8, 128), axis=0)

    for l in range(LV):
        for copy in levels[l]:
            copy.wait()

        def window(ref, first):
            return lambda k: [ref[k, l, u, first : EXT - first] for u in range(2)]

        def still(ref, first):
            return [ref[l, u, first : EXT - first] for u in range(2)]

        def weights(first):
            def at(k):
                got = []
                for u in range(2):
                    left, right = get_edges(ra, rb, (k, l, u), h)
                    skip = first - 8
                    got.append(
                        jnp.concatenate(
                            [left[skip:16], wsum[k, l, u], right[: 16 - skip]], axis=0
                        )
                    )
                return got

            return at

        n, s = still(cn, 0), still(cs, 0)
        x = None
        for k in reversed(range(STEPS)):
            m = []
            for u in range(2):
                left, right = get_edges(ra, rb, (k, l, u), h)
                lm, rm = left[32:], right[32:]
                w = jnp.concatenate([lm, left[:16], wsum[k, l, u], right[:16], rm], axis=0)
                lm, rm = pltpu.roll(lm, 4, 0), pltpu.roll(rm, 4, 0)
                v = jnp.concatenate([lm, left[16:32], vsum[k, l, u], right[16:32], rm], axis=0)
                m.append(v - w * states[k, l, u])
            x = m if x is None else [x[u] + m[u] for u in range(2)]
            x = adjoint(x, window(gains, 0)(k), window(drifts, 0)(k), n, s)
        vectors = [x]
        for first in (8, 16):
            p = [x[u][8 : x[u].shape[0] - 8] for u in range(2)]
            x = hessian(
                p,
                weights(first),
                window(gains, first),
                window(drifts, first),
                still(cn, first),
                still(cs, first),
            )
            vectors.append(x)
        v = [
            [y[u][edge : edge + COL] for u in range(2)] for y, edge in zip(vectors, (24, 16, 8))
        ]
        for i, (a, b) in enumerate(((0, 0), (0, 1), (1, 1), (0, 2), (1, 2))):
            for u in range(2):
                sums[i] = sums[i] + fold(v[a][u], v[b][u])
        for i in range(3):
            for u in range(2):
                out[i * 3 + l, u] = v[i][u]
    lane = lanes((1, 128))
    table = jnp.zeros((1, 128), F32)
    for i in range(5):
        whole = jnp.sum(jnp.sum(sums[i], axis=0, keepdims=True), axis=1, keepdims=True)
        table = jnp.where(lane == i, whole, table)
    table_ref[...] = jnp.broadcast_to(table, (ALL, 128))


def turn_kernel(x, keep, give):
    h = half()
    for f in range(9):
        t = jnp.concatenate([x[f, 0], x[f, 1]], axis=0).T
        for n in range(4):
            first, second = t[n * 32 : n * 32 + 16], t[n * 32 + 16 : n * 32 + 32]
            keep[n, f], give[n, f] = sort_halves(h, first, second)


def merge_out_kernel(keep, got, *outs):
    h = half()
    x = lax.axis_index("lat") >> 1
    low = lanes((16, 128)) < 64
    for t, out in enumerate(outs):
        for f in range(9):
            x0, x1 = sort_halves(h, keep[x ^ t, f], got[x ^ t, f])
            out[f, pl.ds(0, 16, stride=2), :] = jnp.where(low, x0, pltpu.roll(x1, 64, 1))
            out[f, pl.ds(1, 16, stride=2), :] = jnp.where(low, pltpu.roll(x0, 64, 1), x1)


def final_kernel(parts, *refs):
    *xs, increment, residual = refs
    total = jnp.sum(parts[...], axis=0, keepdims=True)
    lane = lanes((1, 128))
    pick = lambda i: jnp.sum(jnp.where(lane == i, total, 0.0), axis=1, keepdims=True)
    a00, a01, a11, a02, a12 = [jnp.broadcast_to(pick(i), (1, 128)) for i in range(5)]
    alpha = a00 / a01
    new = a00 - 2.0 * alpha * a01 + alpha * alpha * a11
    keep1 = 1.0 + new / a00
    curve = keep1 * (keep1 * a01 - alpha * (a02 + a11)) + alpha * alpha * a12
    second = new / curve
    a = alpha + second * keep1
    b = alpha * second
    mine = lax.axis_index("lat") >> 1
    for t, x in enumerate(xs):
        for l in range(LV):
            v0, v1, v2 = x[l], x[3 + l], x[6 + l]
            level = 3 * (mine ^ t) + l
            increment[level] = a * v0 - b * v1
            residual[level] = v0 - a * v1 + b * v2


VM = pl.BlockSpec(memory_space=pltpu.VMEM)
SM = pl.BlockSpec(memory_space=pltpu.SMEM)
AN = pl.BlockSpec(memory_space=pl.ANY)


def call(kernel, outs, *args, scratch=(), space="v", ins=None):
    shapes = tuple(
        pltpu.VMEM(s, F32) if where == "v" else jax.ShapeDtypeStruct(s, F32)
        for s, where in zip(outs, space * len(outs) if len(space) == 1 else space)
    )
    ins = ins or "v" * len(args)
    args = [
        pltpu.with_memory_space_constraint(a, pltpu.VMEM) if i == "v" else a
        for a, i in zip(args, ins)
    ]
    return make(kernel, shapes, ins, scratch)(*args)


def make(kernel, shapes, ins, scratch):
    return pl.pallas_call(
        kernel,
        out_shape=shapes if len(shapes) > 1 else shapes[0],
        in_specs=[{"s": SM, "a": AN}.get(i, VM) for i in ins],
        out_specs=(VM,) * len(shapes) if len(shapes) > 1 else VM,
        scratch_shapes=list(scratch),
    )


def swap(sa, sb):
    near, far = [], []
    for i in range(LAT):
        for j in range(LON):
            me = i * LON + j
            near.append((me, (i ^ 1) * LON + j))
            other = (j + 1) % LON if i % 2 else (j - 1) % LON
            far.append((me, (i ^ 1) * LON + other))
    rb = lax.ppermute(sb, ("lat", "lon"), far)
    ra = lax.ppermute(sa, ("lat", "lon"), near)
    return ra, rb


def flip(x, bits):
    pairs = [(i * LON + j, (i ^ bits) * LON + j) for i in range(LAT) for j in range(LON)]
    return lax.ppermute(x, ("lat", "lon"), pairs)


def ring(blocks):
    return [blocks[0]] + [flip(blocks[t], 2 * t) for t in range(1, 4)]


def on_device(
    background, wind_lon, wind_lat, obs_value, obs_weight, obs_tile, obs_cell, obs_step, obs_count
):
    both = ("lat", "lon")
    plane = (LV, 2, EXT, 128)
    middle = (LV, 2, COL, 128)

    group = (4, 9, 16, 128)
    keep, give = call(prep_kernel, [group] * 2, background, wind_lon, wind_lat, ins="hhh")
    got = flip(give, 1)
    fold = lambda a: a.reshape(16, 128)
    packed = call(
        pack_kernel,
        [(ALL, 8, 128)],
        obs_count,
        fold(obs_tile),
        fold(obs_cell),
        fold(obs_step),
        fold(obs_value),
        fold(obs_weight),
        ins="shhhhh",
        scratch=[
            pltpu.VMEM((9, 16, 128), F32),
            pltpu.VMEM((2048, 128), BF16),
            pltpu.VMEM((2048, 256), F32),
            pltpu.VMEM((1024, 256), F32),
            pltpu.VMEM((1024, 2048), BF16),
            pltpu.VMEM((256, 2048), BF16),
        ],
    )
    arrived = lax.all_to_all(packed, both, 0, 0, tiled=True)
    blocks = ring(call(merge_in_kernel, [(2, 9, 16, 128)] * 4, keep, got))
    fields, sa, sb = call(
        recv_kernel,
        [(9, 2, COL, 128)] + [(9, 2, EDGE, 128)] * 2,
        *blocks,
        space="hvv",
        scratch=[pltpu.VMEM((9, 128, 128), F32)],
    )
    ra, rb = swap(sa, sb)
    wsum, vsum, sa, sb = call(
        scatter_kernel,
        [(STEPS,) + middle] * 2 + [(STEPS, LV, 2, SLAB, 128)] * 2,
        arrived,
        space="hhvv",
        scratch=[
            pltpu.VMEM((4, 256, 128), F32),
            pltpu.VMEM((7, SEG, 128), F32),
            pltpu.VMEM((5 * LV * COL, GROUP * 128), BF16),
            pltpu.VMEM((256, GROUP * 128), BF16),
            pltpu.VMEM((STEPS * 5 * LV * COL, 256), F32),
        ],
    )
    wa, wb = swap(sa, sb)
    coefs = call(
        forward_kernel, [(STEPS,) + plane] * 3 + [plane] * 2, fields, ra, rb, ins="hvv", space="h"
    )
    big = pltpu.VMEM((STEPS,) + plane, F32)
    mid = pltpu.VMEM((STEPS,) + middle, F32)
    small = pltpu.VMEM(plane, F32)
    vectors, table = call(
        core_kernel,
        [(9, 2, COL, 128), (ALL, 128)],
        wa,
        wb,
        wsum,
        vsum,
        *coefs,
        ins="vv" + "a" * 7,
        scratch=[mid, mid, big, big, big, small, small, pltpu.SemaphoreType.DMA((LV, 7))],
    )
    keep, give = call(turn_kernel, [group] * 2, vectors)
    got = flip(give, 1)
    parts = lax.all_to_all(table, both, 0, 0, tiled=True)
    blocks = ring(call(merge_out_kernel, [(9, 32, 128)] * 4, keep, got))
    return call(final_kernel, [(12, 32, 128)] * 2, parts, *blocks, space="h")


def solution(mesh):
    grid = P(None, "lat", "lon")
    flat = P(("lat", "lon"))

    return jax.shard_map(
        on_device,
        mesh=mesh,
        in_specs=(grid, grid, grid, flat, flat, P(("lat", "lon"), None), flat, flat, flat),
        out_specs=(grid, grid),
        check_vma=False,
    )
```

```python
import jax
import jax.numpy as jnp
from jax import lax
from jax.experimental import pallas as pl
from jax.experimental.pallas import tpu as pltpu
from jax.sharding import PartitionSpec as P


LAT = 8
LON = 16
ALL = 128
STEPS = 4
LV = 3
COL = 64
EDGE = 24
EXT = COL + 2 * EDGE
SLAB = 40
MOST = 256
ROOM = 64
GROUP = 4
F32 = jnp.float32
BF16 = jnp.bfloat16
I32 = jnp.int32


def lanes(shape):
    return lax.broadcasted_iota(I32, shape, len(shape) - 1)


def sublanes(shape):
    return lax.broadcasted_iota(I32, shape, len(shape) - 2)


def half():
    return lax.rem(lax.axis_index("lat"), 2)


def sort_halves(h, x, y):
    first = jnp.full(x.shape, h, I32) == 0
    return jnp.where(first, x, y), jnp.where(first, y, x)


def prep_kernel(bg, wl, wt, keep, give):
    low = lanes((16, 128)) < 64
    h = half()
    for f, ref in enumerate((bg, wl, wt)):
        for level in range(12):
            q, l = level // 3, level % 3
            even = ref[level, pl.ds(0, 16, stride=2), :]
            odd = ref[level, pl.ds(1, 16, stride=2), :]
            x = jnp.where(low, even, pltpu.roll(odd, 64, 1))
            y = jnp.where(low, pltpu.roll(even, 64, 1), odd)
            keep[q, f * 3 + l], give[q, f * 3 + l] = sort_halves(h, x, y)


def merge_in_kernel(keep, got, *outs):
    h = half()
    x = lax.axis_index("lat") >> 1
    for t, out in enumerate(outs):
        out[h] = keep[x ^ t]
        out[1 - h] = got[x ^ t]


def put_edges(sa, sb, index, lo, hi, h):
    sa[index], sb[index] = sort_halves(h, hi, lo)


def get_edges(ra, rb, index, h):
    return sort_halves(h, rb[index], ra[index])


def recv_kernel(*refs):
    *xs, center, sa, sb, buf = refs
    h = half()
    mine = lax.axis_index("lat") >> 1
    for t, x in enumerate(xs):
        for c in range(2):
            at = pl.ds(pl.multiple_of((mine ^ t) * 32 + c * 16, 16), 16)
            for f in range(9):
                buf[f, at, :] = x[c, f]
    for f in range(9):
        t = buf[f].T
        for u in range(2):
            center[f, u] = t[u * 64 : u * 64 + 64]
            lo = t[u * 64 : u * 64 + EDGE]
            hi = t[u * 64 + COL - EDGE : u * 64 + COL]
            put_edges(sa, sb, (f, u), lo, hi, h)


def up(x):
    return pltpu.roll(x, x.shape[0] - 1, 0)


def down(x):
    return pltpu.roll(x, 1, 0)


def north(e, o):
    return pltpu.roll(o, 1, 1), e


def south(e, o):
    return o, pltpu.roll(e, 127, 1)


def forward_kernel(center, ra, rb, states, gains, drifts, cn, cs):
    h = half()
    lane = lanes((EXT, 128))

    def ext(f, u):
        left, right = get_edges(ra, rb, (f, u), h)
        return jnp.concatenate([left, center[f, u], right], axis=0)

    for l in range(LV):
        s = [ext(l, u) for u in range(2)]
        wl = [ext(3 + l, u) for u in range(2)]
        wt = [ext(6 + l, u) for u in range(2)]
        n = [0.08 + 0.5 * wt[u] for u in range(2)]
        d = [0.08 - 0.5 * wt[u] for u in range(2)]
        n[0] = jnp.where(lane == 0, 0.0, n[0])
        d[1] = jnp.where(lane == 127, 0.0, d[1])
        for u in range(2):
            cn[l, u] = n[u]
            cs[l, u] = d[u]
        for k in range(STEPS):
            no, so = north(*s), south(*s)
            new = []
            for u in range(2):
                hi, lo = up(s[u]), down(s[u])
                drift = 0.5 * wl[u] + 0.1 * s[u]
                gains[k, l, u] = 0.68 - 0.1 * (hi - lo)
                drifts[k, l, u] = drift
                new.append(
                    0.68 * s[u] + 0.08 * (hi + lo) - drift * (hi - lo) + n[u] * no[u] + d[u] * so[u]
                )
            s = new
            for u in range(2):
                states[k, l, u] = s[u]


def tangent(e, g, d, n, s):
    no, so = north(*e), south(*e)
    out = []
    for u in range(2):
        hi, lo = up(e[u]), down(e[u])
        out.append(g[u] * e[u] + 0.08 * (hi + lo) - d[u] * (hi - lo) + n[u] * no[u] + s[u] * so[u])
    return out


def adjoint(x, g, d, n, s):
    no = north(s[0] * x[0], s[1] * x[1])
    so = south(n[0] * x[0], n[1] * x[1])
    out = []
    for u in range(2):
        flow = d[u] * x[u]
        wide = 0.08 * x[u]
        out.append(g[u] * x[u] + up(wide + flow) + down(wide - flow) + no[u] + so[u])
    return out


def line(x):
    return jnp.broadcast_to(x, (16, 128)).astype(BF16)


def times(hot, scale):
    return (hot.reshape(-1, 16, 128) * scale[None]).reshape(-1, 128)


def pack_kernel(count, first, tile, cell, step, value, weight, out, over, *scratch):
    rows, member, counted, acc, left, right = scratch
    shape = (16, 128)
    live = sublanes(shape) * 128 + lanes(shape) < jnp.broadcast_to(count[...], shape)
    c, t = cell[...], tile[...]
    level = c >> 12
    q = (level >= 3).astype(I32) + (level >= 6).astype(I32) + (level >= 9).astype(I32)
    row = (c & 4095) >> 7
    col = c & 127
    lat = (t >> 4) * 32 + row
    dest = (2 * q + (col >> 6)) * LON + (t & 15)
    w = jnp.where(live, weight[...], 0.0)
    w0 = w.astype(BF16).astype(F32)
    w1 = (w - w0).astype(BF16).astype(F32)
    wv = (w0 + w1) * value[...]
    v0 = wv.astype(BF16).astype(F32)
    v1 = (wv - v0).astype(BF16).astype(F32)
    rows[0] = jnp.where(live, dest, -1).astype(F32)
    rows[1] = (((level - 3 * q) * 64 + (col & 63)) * 256).astype(F32)
    rows[2] = ((lat & 1) * 128 + (lat >> 1)).astype(F32)
    rows[3] = step[...].astype(F32)
    rows[4] = w0
    rows[5] = w1
    rows[6] = v0
    rows[7] = v1
    rows[8] = wv - v0 - v1
    square = (128, 256)
    before = ((sublanes(square) < lanes(square)) | (lanes(square) >= 128)).astype(F32).astype(BF16)
    ids = sublanes((128, 128)).astype(F32)
    for b in range(16):
        at = slice(b * 128, b * 128 + 128)
        hot = jnp.where(ids == rows[0, b : b + 1, :], 1.0, 0.0).astype(BF16)
        member[at, :] = hot
        for p in range(8):
            left[p * 128 : p * 128 + 128, at] = times(hot, line(rows[1 + p, b : b + 1, :]))
    counted[...] = jnp.dot(member[...], before, preferred_element_type=F32)
    base = jnp.zeros((128, 128), F32)
    place = (sublanes((ROOM, 128)) + jnp.broadcast_to(first[...], (ROOM, 128))).astype(F32)
    for b in range(16):
        at = slice(b * 128, b * 128 + 128)
        mine = ids == rows[0, b : b + 1, :]
        rank = jnp.where(mine, counted[at, :128] + base, 0.0)
        rank = jnp.sum(rank, axis=0, keepdims=True)
        base = base + counted[at, 128:]
        hot = jnp.where(place == rank, 1.0, 0.0).astype(BF16)
        right[:ROOM, at] = hot
        right[ROOM:, at] = hot
    acc[...] = lax.dot_general(
        left[...], right[...], (((1,), (1,)), ((), ())), preferred_element_type=F32
    )
    part = lambda *pieces: sum(acc[p * 128 : p * 128 + 128, :] for p in pieces)
    low = lanes((128, 128)) < ROOM
    out[:, 0, :] = jnp.where(low, part(0, 1), part(2))
    out[:, 1, :] = jnp.where(low, part(3, 4), part(5, 6, 7))
    longest = jnp.max(jnp.max(base, axis=0, keepdims=True), axis=1, keepdims=True)
    over[...] = jnp.broadcast_to(jnp.where(longest > ROOM, 1.0, 0.0), (8, 128))


def scatter_kernel(x, wsum, vsum, sa, sb, xt, sorted_, at, bt, acc):
    h = half()
    acc[...] = jnp.zeros_like(acc)
    for pair in range(2):
        xt[pair] = x[:, pair, :].T
    block = (ROOM, 128)
    place = sublanes(block)
    square = (ROOM, ROOM)
    before = (lanes(square) < sublanes(square)).astype(F32).astype(BF16)
    row_ids = sublanes((LV * COL, 128))
    lat_ids = sublanes((256, 128))

    def segment():
        part = lambda ch: xt[ch // 2, ch % 2 * ROOM : ch % 2 * ROOM + ROOM, :]
        step = part(1)
        for k in range(STEPS):
            valid = jnp.where(step == k + 1.0, 1.0, 0.0)
            count = jnp.sum(valid, axis=0, keepdims=True)
            ahead = jnp.dot(before, valid.astype(BF16), preferred_element_type=F32).astype(I32)
            shift = jnp.where(step == k + 1.0, place - ahead, 0)
            moved = [part(0), part(2), part(3)]
            for bit in (1, 2, 4, 8, 16, 32):
                go = shift & bit
                come = pltpu.roll(go, ROOM - bit, 0) != 0
                moved = [jnp.where(come, pltpu.roll(y, ROOM - bit, 0), y) for y in moved]
                shift = jnp.where(
                    come, pltpu.roll(shift, ROOM - bit, 0), jnp.where(go != 0, 0, shift)
                )
            there = place < count.astype(I32)
            cell = moved[0].astype(I32)
            w = jnp.where(there, moved[1], 0.0)
            v = jnp.where(there, moved[2], 0.0)
            w0 = w.astype(BF16).astype(F32)
            v0 = v.astype(BF16).astype(F32)
            v1 = (v - v0).astype(BF16).astype(F32)
            pieces = ((cell >> 8).astype(F32), (cell & 255).astype(F32), w0, w - w0, v0, v1, v - v0 - v1)
            for n, piece in enumerate(pieces):
                sorted_[n] = piece
            longest = jnp.max(count).astype(I32)

            def group(g, carry):
                for r in range(GROUP):
                    cols = slice(r * 128, r * 128 + 128)
                    get = lambda n: sorted_[n, pl.ds(g * GROUP + r, 1), :]
                    hot = jnp.where(row_ids == get(0).astype(I32), 1.0, 0.0).astype(BF16)
                    for p in range(5):
                        at[p * 192 : p * 192 + 192, cols] = times(hot, line(get(2 + p)))
                    bt[:, cols] = jnp.where(lat_ids == get(1).astype(I32), 1.0, 0.0).astype(BF16)
                acc[k * 960 : k * 960 + 960, :] += lax.dot_general(
                    at[...], bt[...], (((1,), (1,)), ((), ())), preferred_element_type=F32
                )
                return carry

            lax.fori_loop(0, (longest + GROUP - 1) // GROUP, group, 0)

    segment()
    for k in range(STEPS):
        for l in range(LV):
            for u in range(2):
                top = k * 960 + l * COL

                def take(p):
                    return acc[top + p * 192 : top + p * 192 + COL, u * 128 : u * 128 + 128]

                w = take(0) + take(1)
                v = take(2) + take(3) + take(4)
                wsum[k, l, u] = w
                vsum[k, l, u] = v
                put_slabs(sa, sb, (k, l, u), w, v, h)


def put_slabs(sa, sb, index, w, v, h):
    low = sublanes((8, 128)) < 4
    mix = jnp.where(low, w[16:24], pltpu.roll(v[16:24], 4, 0))
    lo = jnp.concatenate([w[:16], v[:16], mix], axis=0)
    mix = jnp.where(low, pltpu.roll(v[40:48], 4, 0), w[40:48])
    hi = jnp.concatenate([w[48:], v[48:], mix], axis=0)
    put_edges(sa, sb, index, lo, hi, h)


def slab_kernel(wsum, vsum, sa, sb):
    h = half()
    for k in range(STEPS):
        for l in range(LV):
            for u in range(2):
                put_slabs(sa, sb, (k, l, u), wsum[k, l, u], vsum[k, l, u], h)


def fetch(sources, buffers, sems):
    levels = []
    for l in range(LV):
        copies = []
        for i, (src, dst) in enumerate(zip(sources, buffers)):
            at = (slice(None), l) if len(src.shape) == 5 else l
            copies.append(pltpu.make_async_copy(src.at[at], dst.at[at], sems.at[l, i]))
        levels.append(copies)
        for copy in copies:
            copy.start()
    return levels


def hessian(p, wide, gains, drifts, n, s):
    e, seen = p, []
    for k in range(STEPS):
        e = tangent(e, gains(k), drifts(k), n, s)
        w = wide(k)
        seen.append([w[u] * e[u] for u in range(2)])
    x = None
    for k in reversed(range(STEPS)):
        x = seen[k] if x is None else [x[u] + seen[k][u] for u in range(2)]
        x = adjoint(x, gains(k), drifts(k), n, s)
    return [p[u] + x[u] for u in range(2)]


def core_kernel(
    over, ra, rb, w_in, v_in, states_in, gains_in, drifts_in, cn_in, cs_in, out, table_ref, *scratch
):
    *buffers, sems = scratch
    h = half()
    levels = fetch((w_in, v_in, states_in, gains_in, drifts_in, cn_in, cs_in), buffers, sems)
    wsum, vsum, states, gains, drifts, cn, cs = buffers
    sums = [jnp.zeros((8, 128), F32) for _ in range(5)]

    def fold(a, b):
        prod = a * b
        return jnp.sum(prod.reshape(8, 8, 128), axis=0)

    for l in range(LV):
        for copy in levels[l]:
            copy.wait()

        def window(ref, first):
            return lambda k: [ref[k, l, u, first : EXT - first] for u in range(2)]

        def still(ref, first):
            return [ref[l, u, first : EXT - first] for u in range(2)]

        def weights(first):
            def at(k):
                got = []
                for u in range(2):
                    left, right = get_edges(ra, rb, (k, l, u), h)
                    skip = first - 8
                    got.append(
                        jnp.concatenate(
                            [left[skip:16], wsum[k, l, u], right[: 16 - skip]], axis=0
                        )
                    )
                return got

            return at

        n, s = still(cn, 0), still(cs, 0)
        x = None
        for k in reversed(range(STEPS)):
            m = []
            for u in range(2):
                left, right = get_edges(ra, rb, (k, l, u), h)
                lm, rm = left[32:], right[32:]
                w = jnp.concatenate([lm, left[:16], wsum[k, l, u], right[:16], rm], axis=0)
                lm, rm = pltpu.roll(lm, 4, 0), pltpu.roll(rm, 4, 0)
                v = jnp.concatenate([lm, left[16:32], vsum[k, l, u], right[16:32], rm], axis=0)
                m.append(v - w * states[k, l, u])
            x = m if x is None else [x[u] + m[u] for u in range(2)]
            x = adjoint(x, window(gains, 0)(k), window(drifts, 0)(k), n, s)
        vectors = [x]
        for first in (8, 16):
            p = [x[u][8 : x[u].shape[0] - 8] for u in range(2)]
            x = hessian(
                p,
                weights(first),
                window(gains, first),
                window(drifts, first),
                still(cn, first),
                still(cs, first),
            )
            vectors.append(x)
        v = [
            [y[u][edge : edge + COL] for u in range(2)] for y, edge in zip(vectors, (24, 16, 8))
        ]
        for i, (a, b) in enumerate(((0, 0), (0, 1), (1, 1), (0, 2), (1, 2))):
            for u in range(2):
                sums[i] = sums[i] + fold(v[a][u], v[b][u])
        for i in range(3):
            for u in range(2):
                out[i * 3 + l, u] = v[i][u]
    lane = lanes((1, 128))
    table = jnp.zeros((1, 128), F32)
    for i in range(5):
        whole = jnp.sum(jnp.sum(sums[i], axis=0, keepdims=True), axis=1, keepdims=True)
        table = jnp.where(lane == i, whole, table)
    table = jnp.where(lane == 5, over[:1], table)
    table_ref[...] = jnp.broadcast_to(table, (ALL, 128))


def turn_kernel(x, keep, give):
    h = half()
    for f in range(9):
        t = jnp.concatenate([x[f, 0], x[f, 1]], axis=0).T
        for n in range(4):
            first, second = t[n * 32 : n * 32 + 16], t[n * 32 + 16 : n * 32 + 32]
            keep[n, f], give[n, f] = sort_halves(h, first, second)


def merge_out_kernel(keep, got, *outs):
    h = half()
    x = lax.axis_index("lat") >> 1
    low = lanes((16, 128)) < 64
    for t, out in enumerate(outs):
        for f in range(9):
            x0, x1 = sort_halves(h, keep[x ^ t, f], got[x ^ t, f])
            out[f, pl.ds(0, 16, stride=2), :] = jnp.where(low, x0, pltpu.roll(x1, 64, 1))
            out[f, pl.ds(1, 16, stride=2), :] = jnp.where(low, pltpu.roll(x0, 64, 1), x1)


def final_kernel(parts, *refs):
    *xs, increment, residual = refs
    total = jnp.sum(parts[...], axis=0, keepdims=True)
    lane = lanes((1, 128))
    pick = lambda i: jnp.sum(jnp.where(lane == i, total, 0.0), axis=1, keepdims=True)
    a00, a01, a11, a02, a12 = [jnp.broadcast_to(pick(i), (1, 128)) for i in range(5)]
    alpha = a00 / a01
    new = a00 - 2.0 * alpha * a01 + alpha * alpha * a11
    keep1 = 1.0 + new / a00
    curve = keep1 * (keep1 * a01 - alpha * (a02 + a11)) + alpha * alpha * a12
    second = new / curve
    a = alpha + second * keep1
    b = alpha * second
    mine = lax.axis_index("lat") >> 1
    for t, x in enumerate(xs):
        for l in range(LV):
            v0, v1, v2 = x[l], x[3 + l], x[6 + l]
            level = 3 * (mine ^ t) + l
            increment[level] = a * v0 - b * v1
            residual[level] = v0 - a * v1 + b * v2


VM = pl.BlockSpec(memory_space=pltpu.VMEM)
SM = pl.BlockSpec(memory_space=pltpu.SMEM)
AN = pl.BlockSpec(memory_space=pl.ANY)


def call(kernel, outs, *args, scratch=(), space="v", ins=None):
    shapes = tuple(
        pltpu.VMEM(s, F32) if where == "v" else jax.ShapeDtypeStruct(s, F32)
        for s, where in zip(outs, space * len(outs) if len(space) == 1 else space)
    )
    ins = ins or "v" * len(args)
    args = [
        pltpu.with_memory_space_constraint(a, pltpu.VMEM) if i == "v" else a
        for a, i in zip(args, ins)
    ]
    return make(kernel, shapes, ins, scratch)(*args)


def make(kernel, shapes, ins, scratch):
    return pl.pallas_call(
        kernel,
        out_shape=shapes if len(shapes) > 1 else shapes[0],
        in_specs=[{"s": SM, "a": AN}.get(i, VM) for i in ins],
        out_specs=(VM,) * len(shapes) if len(shapes) > 1 else VM,
        scratch_shapes=list(scratch),
    )


def swap(sa, sb):
    near, far = [], []
    for i in range(LAT):
        for j in range(LON):
            me = i * LON + j
            near.append((me, (i ^ 1) * LON + j))
            other = (j + 1) % LON if i % 2 else (j - 1) % LON
            far.append((me, (i ^ 1) * LON + other))
    rb = lax.ppermute(sb, ("lat", "lon"), far)
    ra = lax.ppermute(sa, ("lat", "lon"), near)
    return ra, rb


def flip(x, bits):
    pairs = [(i * LON + j, (i ^ bits) * LON + j) for i in range(LAT) for j in range(LON)]
    return lax.ppermute(x, ("lat", "lon"), pairs)


def ring(blocks):
    return [blocks[0]] + [flip(blocks[t], 2 * t) for t in range(1, 4)]


def pack(observed):
    return call(
        pack_kernel,
        [(ALL, 2, 128), (8, 128)],
        *observed,
        ins="h" * 7,
        scratch=[
            pltpu.VMEM((9, 16, 128), F32),
            pltpu.VMEM((2048, 128), BF16),
            pltpu.VMEM((2048, 256), F32),
            pltpu.VMEM((1024, 128), F32),
            pltpu.VMEM((1024, 2048), BF16),
            pltpu.VMEM((128, 2048), BF16),
        ],
    )


def scatter(arrived):
    return call(
        scatter_kernel,
        [(STEPS, LV, 2, COL, 128)] * 2 + [(STEPS, LV, 2, SLAB, 128)] * 2,
        arrived,
        space="hhvv",
        scratch=[
            pltpu.VMEM((2, 128, 128), F32),
            pltpu.VMEM((7, ROOM, 128), F32),
            pltpu.VMEM((5 * LV * COL, GROUP * 128), BF16),
            pltpu.VMEM((256, GROUP * 128), BF16),
            pltpu.VMEM((STEPS * 5 * LV * COL, 256), F32),
        ],
    )


BOTH = ("lat", "lon")
PLANE = (LV, 2, EXT, 128)
MIDDLE = (LV, 2, COL, 128)
SPLIT = (4, 9, 16, 128)


def solve(over, wsum, vsum, wa, wb, coefs):
    big = pltpu.VMEM((STEPS,) + PLANE, F32)
    mid = pltpu.VMEM((STEPS,) + MIDDLE, F32)
    small = pltpu.VMEM(PLANE, F32)
    vectors, table = call(
        core_kernel,
        [(9, 2, COL, 128), (ALL, 128)],
        over,
        wa,
        wb,
        wsum,
        vsum,
        *coefs,
        ins="vvv" + "a" * 7,
        scratch=[mid, mid, big, big, big, small, small, pltpu.SemaphoreType.DMA((LV, 7))],
    )
    keep, give = call(turn_kernel, [SPLIT] * 2, vectors)
    got = flip(give, 1)
    parts = lax.all_to_all(table, BOTH, 0, 0, tiled=True)
    blocks = ring(call(merge_out_kernel, [(9, 32, 128)] * 4, keep, got))
    increment, residual = call(
        final_kernel, [(12, 32, 128)] * 2, parts, *blocks, space="h"
    )
    return increment, residual, parts


def every_window(observed, coefs):
    def window(i, sums):
        first = jnp.full((1, 1), i * ROOM, I32)
        packed, _ = pack(observed[:1] + (first,) + observed[2:])
        arrived = lax.all_to_all(packed, BOTH, 0, 0, tiled=True)
        w, v, _, _ = scatter(arrived)
        return sums[0] + w, sums[1] + v

    zeros = jnp.zeros((STEPS,) + MIDDLE, F32)
    wsum, vsum = lax.fori_loop(0, MOST // ROOM, window, (zeros, zeros))
    sa, sb = call(slab_kernel, [(STEPS, LV, 2, SLAB, 128)] * 2, wsum, vsum, ins="hh")
    wa, wb = swap(sa, sb)
    increment, residual, _ = solve(jnp.zeros((8, 128), F32), wsum, vsum, wa, wb, coefs)
    return increment, residual


def on_device(
    background, wind_lon, wind_lat, obs_value, obs_weight, obs_tile, obs_cell, obs_step, obs_count
):
    both = ("lat", "lon")
    plane = (LV, 2, EXT, 128)

    group = (4, 9, 16, 128)
    keep, give = call(prep_kernel, [group] * 2, background, wind_lon, wind_lat, ins="hhh")
    got = flip(give, 1)
    fold = lambda a: a.reshape(16, 128)
    observed = (
        obs_count.reshape(1, 1),
        jnp.zeros((1, 1), I32),
        fold(obs_tile),
        fold(obs_cell),
        fold(obs_step),
        fold(obs_value),
        fold(obs_weight),
    )
    packed, over = pack(observed)
    arrived = lax.all_to_all(packed, both, 0, 0, tiled=True)
    blocks = ring(call(merge_in_kernel, [(2, 9, 16, 128)] * 4, keep, got))
    fields, sa, sb = call(
        recv_kernel,
        [(9, 2, COL, 128)] + [(9, 2, EDGE, 128)] * 2,
        *blocks,
        space="hvv",
        scratch=[pltpu.VMEM((9, 128, 128), F32)],
    )
    ra, rb = swap(sa, sb)
    wsum, vsum, sa, sb = scatter(arrived)
    wa, wb = swap(sa, sb)
    coefs = call(
        forward_kernel, [(STEPS,) + plane] * 3 + [plane] * 2, fields, ra, rb, ins="hvv", space="h"
    )
    increment, residual, parts = solve(over, wsum, vsum, wa, wb, coefs)
    crowded = jnp.sum(parts[:, 5]) > 0.5
    return lax.cond(
        crowded, lambda: every_window(observed, coefs), lambda: (increment, residual)
    )


def solution(mesh):
    grid = P(None, "lat", "lon")
    flat = P(("lat", "lon"))

    return jax.shard_map(
        on_device,
        mesh=mesh,
        in_specs=(grid, grid, grid, flat, flat, P(("lat", "lon"), None), flat, flat, flat),
        out_specs=(grid, grid),
        check_vma=False,
    )
```
